32 devices in a mesh: expert: 8 (over y, x, core), tensor: 4 (over z).
Axes of the slice: x: 2, y: 2, z: 4, core: 2. Of those that a mesh axis runs over, the one named last changes fastest.
Arguments:
- tokens: bfloat16 [4096, 2560], P(('expert', 'tensor')), may hold values from -6 to 6
- expert_ids: int32 [4096, 1], P(('expert', 'tensor')), may hold values from 0 to 7; in each aligned block of 512 rows (0 to 511, 512 to 1023, ...) at most 128 rows name the same one
- gates: float32 [4096], P(('expert', 'tensor')), may hold values from 0.3 to 3
- w_gate: bfloat16 [8, 2560, 4096], P('expert', None, 'tensor'), may hold values from -0.125 to 0.125
- w_up: bfloat16 [8, 2560, 4096], P('expert', None, 'tensor'), may hold values from -0.125 to 0.125
- w_down: bfloat16 [8, 4096, 2560], P('expert', 'tensor'), may hold values from -0.09375 to 0.09375
- s_gate: bfloat16 [2560, 4096], P('expert', 'tensor'), may hold values from -0.125 to 0.125
- s_up: bfloat16 [2560, 4096], P('expert', 'tensor'), may hold values from -0.125 to 0.125
- s_down: bfloat16 [4096, 2560], P('tensor', 'expert'), may hold values from -0.09375 to 0.09375
Outputs:
- mixed: bfloat16 [4096, 2560], P(('expert', 'tensor'))
The draws below stay inside these ranges and needn't reach their ends.
Inputs may be any that keep to these rules, and one draw needn't show every extreme that they name: `expert_ids`: in each aligned block of 512 tokens no expert is named by more than 128 tokens, and some block has an expert named by exactly 128 tokens.
All inputs are finite; a program needn't handle non-finite values.
Results may differ from the reference program's by a relative error of at most 0.013.
Values may be sent and summed in bfloat16 or wider, within the bound.
No kernel may reach another device: no remote copies, remote signals or barrier semaphores. Data moves between devices by JAX's collectives and lax.ppermute only.
A program may use at most 128 MiB of HBM per device.

```python
import math
import jax
import jax.numpy as jnp
import numpy as np
from jax import lax

D = 2560
FF_EXPERT = 4096
FF_SHARED = 4096
TOK_DEV = 128
EXPERTS = 8
TOKENS = 4096
CAP = 128
N_TENSOR = 4


def steps_of(stream_key, extent, shards, least, top_value):
    def one(axis_at, blocks):
        heights = jax.random.uniform(jax.random.fold_in(jax.random.fold_in(stream_key, 6), axis_at), (blocks,), jnp.float32, least / len(shards), top_value / len(shards))
        return jnp.repeat(jnp.exp(heights), extent[axis_at] // blocks).reshape((-1,) + (1,) * (len(extent) - axis_at - 1))

    level = one(*shards[0])
    for cut in shards[1:]:
        level = level * one(*cut)
    return level


def deal_out(rng, own, number, rows, count, top, reach, skew):
    sequence = jax.random.permutation(rng, count)
    crowded, common = shares(count, rows * top, reach, skew, True), shares(count, rows * top, reach, skew, False)
    places = jnp.arange(count)

    def named(lengths, turn):
        used = int((lengths > 0).sum())
        fixed = max(1, used // 4)
        shifted = fixed + (places - fixed + turn * (used - fixed)) % max(1, count - fixed)
        return jnp.zeros((count,), jnp.int32).at[sequence[jnp.where(places < fixed, places, shifted)]].set(jnp.asarray(lengths, jnp.int32))

    lengths = jnp.where(number % 4 == 0, named(crowded, number // 4), named(common, number - number // 4 - 1))
    mixed = jax.random.permutation(jax.random.fold_in(own, 3), count)
    source_of, sink = mixed[0:count // 2 * 2:2], mixed[1:count // 2 * 2:2]
    margin = jnp.minimum(lengths[source_of] - 1, reach - lengths[sink]) // 2
    margin = jnp.where((source_of == sequence[0]) | (sink == sequence[0]) | (lengths[sink] == 0), 0, jnp.maximum(margin, 0))
    shifted = jax.random.randint(jax.random.fold_in(own, 4), (count // 2,), 0, 1 << 20) % (margin + 1)
    lengths = lengths.at[source_of].add(-shifted).at[sink].add(shifted)
    members = jnp.searchsorted(jnp.cumsum(lengths), jnp.arange(rows * top), side="right").astype(jnp.int32)
    table = members.reshape(top, rows).T
    table = table[jax.random.permutation(jax.random.fold_in(own, 1), rows)]
    turn = jax.random.randint(jax.random.fold_in(own, 2), (rows, 1), 0, top)
    return jnp.take_along_axis(table, (jnp.arange(top)[None, :] + turn) % top, axis=1)


def shares(number_of, total, limit, skew, full):
    portions = [(1 << 20) // math.isqrt(grade ** skew) + 1 for grade in range(1, number_of + 1)]
    largest = limit if full else min(limit, max(-(-total // number_of), total * portions[0] // sum(portions)))
    least = 1 if total - largest >= number_of - 1 else 0
    counts, spare = [largest] + [least] * (number_of - 1), total - largest - least * (number_of - 1)
    while spare > 0:
        free = [i for i in range(1, number_of) if counts[i] < largest] or [i for i in range(1, number_of) if counts[i] < limit]
        whole, left = sum([portions[i] for i in free]), spare
        for i in free:
            addition = min(limit - counts[i], max(1, left * portions[i] // whole), spare)
            counts[i] = counts[i] + addition
            spare = spare - addition
    return np.array(counts)


def bell_draw(own_key, shape, scale, limit, cuts=(), kind=jnp.bfloat16):
    array = scale * jax.random.normal(own_key, shape, jnp.float32)
    if cuts:
        array = array * steps_of(own_key, shape, cuts, -0.22, 0.18)
    return jnp.clip(array, -limit, limit).astype(kind)


def setup_inputs(seed: int = 0) -> dict:
    key_of = jax.random.split(jax.random.key(seed), 10)
    tokens = bell_draw(key_of[0], (TOKENS, D), 1.0, 6.0, ((0, 32),))
    expert_ids_keys = jax.random.split(jax.random.fold_in(key_of[1], 1), TOKENS // (TOK_DEV * N_TENSOR))
    expert_ids_turns = jax.random.permutation(jax.random.fold_in(key_of[1], 3), TOKENS // (TOK_DEV * N_TENSOR))
    expert_ids = jax.vmap(lambda own, number: deal_out(jax.random.fold_in(key_of[1], 2), own, number, TOK_DEV * N_TENSOR, EXPERTS, 1, CAP, 2))(expert_ids_keys, expert_ids_turns).reshape((TOKENS, 1))
    gates = jnp.clip(jnp.exp(math.log(3.0) - 2.3025851 * jax.random.uniform(key_of[2], (TOKENS,), jnp.float32) ** steps_of(key_of[2], (TOKENS,), ((0, 32),), -0.2, 0.2)), 0.3, 3.0)
    w_gate = bell_draw(key_of[3], (EXPERTS, D, FF_EXPERT), D ** -0.5, 0.125, ((0, 8), (2, 4)))
    w_up = bell_draw(key_of[4], (EXPERTS, D, FF_EXPERT), D ** -0.5, 0.125, ((0, 8), (2, 4)))
    w_down = bell_draw(key_of[5], (EXPERTS, FF_EXPERT, D), FF_EXPERT ** -0.5, 0.09375, ((0, 8), (1, 4)))
    s_gate = bell_draw(key_of[6], (D, FF_SHARED), D ** -0.5, 0.125, ((0, 8), (1, 4)))
    s_up = bell_draw(key_of[7], (D, FF_SHARED), D ** -0.5, 0.125, ((0, 8), (1, 4)))
    s_down = bell_draw(key_of[8], (FF_SHARED, D), FF_SHARED ** -0.5, 0.09375, ((0, 4), (1, 8)))
    return {"tokens": tokens, "expert_ids": expert_ids, "gates": gates, "w_gate": w_gate, "w_up": w_up, "w_down": w_down, "s_gate": s_gate, "s_up": s_up, "s_down": s_down}


def slots_of(ids, experts, cap):
    onehot = (ids[:, None] == jnp.arange(experts, dtype=jnp.int32)[None, :]).astype(jnp.int32)
    before = jnp.cumsum(onehot, axis=0) - onehot
    position = jnp.sum(before * onehot, axis=1)
    return (ids * cap + position).astype(jnp.int32)


def dispatch_rows(rows, slot, total):
    count = rows.shape[0]
    owner = jnp.full((total,), count, jnp.int32).at[slot].set(jnp.arange(count, dtype=jnp.int32))
    padded = jnp.concatenate([rows, jnp.zeros((1, rows.shape[1]), rows.dtype)], axis=0)
    return jnp.take(padded, owner, axis=0)


def swiglu(rows, first, second):
    gate = jnp.dot(rows, first, preferred_element_type=jnp.float32)
    upper = jnp.dot(rows, second, preferred_element_type=jnp.float32)
    return (jax.nn.silu(gate) * upper).astype(jnp.bfloat16)


def block_products(hidden, weight, blocks):
    width = hidden.shape[1] // blocks
    parts = []
    for index in range(blocks):
        parts.append(jnp.dot(hidden[:, index * width:(index + 1) * width], weight[index * width:(index + 1) * width], preferred_element_type=jnp.float32))
    return jnp.stack(parts, axis=1)


def reference(tokens, expert_ids, gates, w_gate, w_up, w_down, s_gate, s_up, s_down):
    group = TOK_DEV * N_TENSOR
    groups = TOKENS // group
    rows = tokens.reshape(groups, group, D)
    ids = expert_ids.reshape(groups, group)
    weights = gates.reshape(groups, group)

    def group_apply(items):
        rows_group, ids_group, gates_group = items
        slot = slots_of(ids_group, EXPERTS, CAP)
        buffers = dispatch_rows(rows_group, slot, EXPERTS * CAP).reshape(EXPERTS, CAP, D)

        def expert_apply(parts):
            x, first, second, third = parts
            return block_products(swiglu(x, first, second), third, N_TENSOR).astype(jnp.bfloat16)

        outputs = lax.map(expert_apply, (buffers, w_gate, w_up, w_down))
        routed = jnp.take(outputs.reshape(EXPERTS * CAP, N_TENSOR, D), slot, axis=0).astype(jnp.float32)
        shared = block_products(swiglu(rows_group, s_gate, s_up), s_down, N_TENSOR)
        terms = (shared + gates_group[:, None, None] * routed).astype(jnp.bfloat16).astype(jnp.float32)
        return jnp.sum(terms, axis=1).astype(jnp.bfloat16)

    return lax.map(group_apply, (rows, ids, weights)).reshape(TOKENS, D)
```

```python
import jax
import jax.numpy as jnp
from jax import lax
from jax.sharding import PartitionSpec as P

CHUNKS = 2
F32 = jnp.float32
BF16 = jnp.bfloat16


def dot(a, b):
    return jnp.dot(a, b, preferred_element_type=F32)


def line_gather(block, count, place):
    up, down, ups, downs = block, block, [], []
    for step in range(1, count):
        up = lax.ppermute(up, "tensor", [(i, i + 1) for i in range(step - 1, count - 1)])
        down = lax.ppermute(down, "tensor", [(i, i - 1) for i in range(1, count - step + 1)])
        ups.append(up)
        downs.append(down)
    parts = [block]
    for back in range(1, count):
        parts.append(jnp.where(place >= back, ups[back - 1], downs[count - back - 1]))
    return jnp.concatenate(parts, axis=0)


def line_scatter(total, count):
    rows = total.shape[0] // count
    part = [total[k * rows:(k + 1) * rows] for k in range(count)]
    up = down = None
    for step in range(1, count):
        first, second = part[step], part[count - step]
        if up is not None:
            first = (first.astype(F32) + up.astype(F32)).astype(BF16)
            second = (second.astype(F32) + down.astype(F32)).astype(BF16)
        up = lax.ppermute(first, "tensor", [(i, i + 1) for i in range(step)])
        down = lax.ppermute(second, "tensor", [(i, i - 1) for i in range(count - step, count)])
    out = part[0].astype(F32)
    if up is not None:
        out = out + up.astype(F32) + down.astype(F32)
    return out.astype(BF16)


def body(tokens, expert_ids, gates, w_gate, w_up, w_down, s_gate, s_up, s_down):
    n_expert = lax.axis_size("expert")
    count = lax.axis_size("tensor")
    place = lax.axis_index("tensor")
    rows, width = tokens.shape
    group = rows * count
    experts = w_gate.shape[0] * n_expert
    cap = 2 * group // experts
    cuts = [width * c // CHUNKS for c in range(CHUNKS + 1)]
    spans = [slice(cuts[c], cuts[c + 1]) for c in range(CHUNKS)]

    inner = s_gate.shape[1]
    s_in = lax.all_gather(jnp.concatenate([s_gate, s_up], axis=1), "expert", axis=0, tiled=True)
    gathered = [line_gather(tokens[:, s], count, place) for s in spans]
    meta = jnp.concatenate([expert_ids.astype(F32).T, gates[None, :]], axis=0)
    meta = lax.all_gather(meta, "tensor", axis=0, tiled=False)[::-1]
    meta = lax.dynamic_slice_in_dim(jnp.concatenate([meta, meta]), count - 1 - place, count)
    ids = meta[:, 0, :].reshape(group).astype(jnp.int32)
    scale = meta[:, 1, :].reshape(group)

    index = jnp.arange(group, dtype=jnp.int32)
    same = (ids[:, None] == ids[None, :]) & (index[None, :] < index[:, None])
    slot = ids * cap + jnp.sum(same.astype(jnp.int32), axis=1)
    places = jnp.arange(experts * cap, dtype=jnp.int32)
    into = (places[:, None] == slot[None, :]).astype(BF16)
    outof = (slot[:, None] == places[None, :]).astype(BF16)

    gate = upper = None
    for s, part in zip(spans, gathered):
        sent = dot(into, part).astype(BF16).reshape(experts, cap, -1)
        got = lax.all_to_all(sent, "expert", split_axis=0, concat_axis=0, tiled=True)
        got = got.reshape(experts * cap, -1)
        g, u = dot(got, w_gate[0, s]), dot(got, w_up[0, s])
        gate, upper = (g, u) if gate is None else (gate + g, upper + u)
    hidden = (jax.nn.silu(gate) * upper).astype(BF16)

    pre = None
    for s, part in zip(spans, gathered):
        term = dot(part, s_in[s])
        pre = term if pre is None else pre + term
    shared = (jax.nn.silu(pre[:, :inner]) * pre[:, inner:]).astype(BF16)
    s_out = lax.all_gather(s_down, "expert", axis=1, tiled=True)

    outs = []
    for s in spans:
        made = dot(hidden, w_down[0, :, s]).astype(BF16).reshape(experts, cap, -1)
        back = lax.all_to_all(made, "expert", split_axis=0, concat_axis=0, tiled=True)
        routed = dot(outof, back.reshape(experts * cap, -1))
        term = (dot(shared, s_out[:, s]) + scale[:, None] * routed).astype(BF16)
        outs.append(line_scatter(term, count))
    return jnp.concatenate(outs, axis=1)


def solution(mesh):
    return jax.shard_map(
        body,
        mesh=mesh,
        in_specs=(
            P(("expert", "tensor"), None),
            P(("expert", "tensor"), None),
            P(("expert", "tensor")),
            P("expert", None, "tensor"),
            P("expert", None, "tensor"),
            P("expert", "tensor", None),
            P("expert", "tensor"),
            P("expert", "tensor"),
            P("tensor", "expert"),
        ),
        out_specs=P(("expert", "tensor"), None),
        check_vma=False,
    )
```

```python
import jax
import jax.numpy as jnp
from jax import lax
from jax.sharding import PartitionSpec as P

F32 = jnp.float32
BF16 = jnp.bfloat16


def dot(a, b):
    return jnp.dot(a, b, preferred_element_type=F32)


def dot_t(a, b):
    return lax.dot_general(a, b, (((1,), (1,)), ((), ())), preferred_element_type=F32)


def after(value, *others):
    return lax.optimization_barrier((value, *others))[0]


def swap(block, axis, bits):
    size = lax.axis_size(axis)
    return lax.ppermute(block, axis, [(i, i ^ bits) for i in range(size)])


def bits_of(number):
    return [1 << b for b in range(number.bit_length()) if number >> b & 1]


def far(offset):
    return len(bits_of(offset >> 1)) > 1


def line_gather(block, count, place, gate=None):
    up, down, ups, downs = block, block, [], []
    for step in range(1, count):
        up = lax.ppermute(up, "tensor", [(i, i + 1) for i in range(step - 1, count - 1)])
        down = lax.ppermute(down, "tensor", [(i, i - 1) for i in range(1, count - step + 1)])
        ups.append(up)
        downs.append(down)
    parts = [block]
    for back in range(1, count):
        parts.append(jnp.where(place >= back, ups[back - 1], downs[count - back - 1]))
    return parts, ups[-2] if count > 2 else ups[-1]


def line_scatter(total, count):
    rows = total.shape[0] // count
    part = [total[k * rows:(k + 1) * rows] for k in range(count)]
    up = down = None
    for step in range(1, count):
        first, second = part[step], part[count - step]
        if up is not None:
            first = (first.astype(F32) + up.astype(F32)).astype(BF16)
            second = (second.astype(F32) + down.astype(F32)).astype(BF16)
        up = lax.ppermute(first, "tensor", [(i, i + 1) for i in range(step)])
        down = lax.ppermute(second, "tensor", [(i, i - 1) for i in range(count - step, count)])
    out = part[0].astype(F32)
    if up is not None:
        out = out + up.astype(F32) + down.astype(F32)
    return out.astype(BF16)


def near_blocks(block, size):
    return {bit: swap(block, "expert", bit) for bit in bits_of((size - 1) & ~1)}


def all_blocks(block, near, size):
    half = block.shape[1] // 2
    held = {0: block, **near}
    for offset in range(2, size, 2):
        if offset in held:
            continue
        low, high = bits_of(offset)[0], bits_of(offset)[-1]
        held[offset] = jnp.concatenate(
            [
                swap(held[offset ^ low][:, :half], "expert", low),
                swap(held[offset ^ high][:, half:], "expert", high),
            ],
            axis=1,
        )
    for offset in range(0, size, 2):
        held[offset + 1] = swap(held[offset], "expert", 1)
    return held


def in_order(held, me):
    rows, columns = held[0].shape
    out = jnp.zeros((rows * len(held), columns), held[0].dtype)
    for offset, block in held.items():
        out = lax.dynamic_update_slice(out, block, ((me ^ offset) * rows, 0))
    return out


def body(tokens, expert_ids, gates, w_gate, w_up, w_down, s_gate, s_up, s_down):
    size = lax.axis_size("expert")
    count = lax.axis_size("tensor")
    me = lax.axis_index("expert")
    place = lax.axis_index("tensor")
    rows, width = tokens.shape
    group = rows * count
    per = w_gate.shape[0]
    experts = per * size
    cap = 2 * group // experts
    half = cap // 2
    cut = width // 2
    spans = [slice(0, cut), slice(cut, width)]
    inner = s_gate.shape[1]

    gates = gates[None, :]
    top = lax.reduce_precision(gates, 8, 7)
    middle = lax.reduce_precision(gates - top, 8, 7)
    notes = jnp.concatenate([expert_ids.astype(F32).T, top, middle, gates - top - middle], axis=0)
    notes = jnp.pad(notes.astype(BF16), ((0, 12), (0, cut - rows)))
    first, mark = line_gather(jnp.concatenate([tokens[:, spans[0]], notes]), count, place)
    s_pair = jnp.concatenate([s_gate, s_up], axis=1)
    near_in = near_blocks(s_pair, size)
    second, _ = line_gather(after(tokens[:, spans[1]], mark), count, place)

    notes = jnp.concatenate([p[rows:rows + 4, :rows] for p in first], axis=1).astype(F32)
    ids = notes[0].astype(jnp.int32)
    scale = notes[1] + notes[2] + notes[3]
    pieces = [jnp.concatenate([p[:rows] for p in first]), jnp.concatenate(second)]

    index = jnp.arange(group, dtype=jnp.int32)
    back = index // rows
    index = jnp.where(back > place, place - back + count, place - back) * rows + index % rows
    same = (ids[:, None] == ids[None, :]) & (index[None, :] < index[:, None])
    spot = jnp.sum(same.astype(jnp.int32), axis=1)
    turned = spot + (place & 1) * half
    turned = jnp.where(turned >= cap, turned - cap, turned)
    base, lengths, total = [], [], 0
    for offset in range(size):
        lengths.append(half if far(offset) else cap)
        base.append(total)
        total += lengths[-1]
    offset_of = ids ^ me
    slot = jnp.full((group,), -1, jnp.int32)
    for offset in range(size):
        value = base[offset] + (turned if far(offset) else spot)
        if far(offset):
            value = jnp.where(turned < half, value, -1)
        slot = jnp.where(offset_of == offset, value, slot)
    places = jnp.arange(total, dtype=jnp.int32)
    into = (places[:, None] == slot[None, :]).astype(BF16)
    outof = (slot[:, None] == places[None, :]).astype(BF16)
    fars = [o for o in range(size) if far(o)]
    nears = [o for o in range(1, size) if not far(o)]
    order = fars + nears[::-1]

    gate = upper = None
    for s, piece in zip(spans, pieces):
        sent = dot(into, piece).astype(BF16)
        got = {0: sent[:cap]}
        for o in order:
            got[o] = swap(sent[base[o]:base[o] + lengths[o]], "expert", o)
        mine = jnp.concatenate([got[o] for o in fars])
        got = jnp.concatenate([got[0]] + [got[o] for o in nears] + [mine, swap(mine, "tensor", 1)])
        g, u = dot(got, w_gate[0, s]), dot(got, w_up[0, s])
        gate, upper = (g, u) if gate is None else (gate + g, upper + u)
    hidden = (jax.nn.silu(gate) * upper).astype(BF16)

    near_in = {k: after(v, got) for k, v in near_in.items()}
    s_in = in_order(all_blocks(s_pair, near_in, size), me)
    s_turned = after(s_down.T, got)
    s_out = in_order(all_blocks(s_turned, near_blocks(s_turned, size), size), me)
    pre = dot(pieces[0], s_in[spans[0]]) + dot(pieces[1], s_in[spans[1]])
    shared = (jax.nn.silu(pre[:, :inner]) * pre[:, inner:]).astype(BF16)

    outs = []
    split = (1 + len(nears)) * cap
    for s in spans:
        made = dot(hidden, w_down[0, :, s])
        theirs = swap(made[total:].astype(BF16), "tensor", 1)
        mine = (made[split:total] + theirs.astype(F32)).astype(BF16)
        made = made.astype(BF16)
        home = {0: made[:cap]}
        for k, o in enumerate(nears):
            home[o] = swap(made[(k + 1) * cap:(k + 2) * cap], "expert", o)
        for k, o in enumerate(fars):
            home[o] = swap(mine[k * half:(k + 1) * half], "expert", o)
        routed = dot(outof, jnp.concatenate([home[o] for o in range(size)]))
        term = (dot_t(shared, s_out[s]) + scale[:, None] * routed).astype(BF16)
        outs.append(line_scatter(term, count))
    return jnp.concatenate(outs, axis=1)


def solution(mesh):
    return jax.shard_map(
        body,
        mesh=mesh,
        in_specs=(
            P(("expert", "tensor"), None),
            P(("expert", "tensor"), None),
            P(("expert", "tensor")),
            P("expert", None, "tensor"),
            P("expert", None, "tensor"),
            P("expert", "tensor", None),
            P("expert", "tensor"),
            P("expert", "tensor"),
            P("tensor", "expert"),
        ),
        out_specs=P(("expert", "tensor"), None),
        check_vma=False,
    )
```

```python
import functools

import jax
import jax.numpy as jnp
from jax import lax
from jax.experimental import pallas as pl
from jax.experimental.pallas import tpu as pltpu
from jax.sharding import PartitionSpec as P


F32 = jnp.float32
BF16 = jnp.bfloat16
LANES = 128
VMEM_BYTES = 56 * 1024 * 1024
VMEM_SPEC = pl.BlockSpec(memory_space=pltpu.VMEM)
ANY_SPEC = pl.BlockSpec(memory_space=pl.ANY)


def dot(a, b):
    return jnp.dot(a, b, preferred_element_type=F32)


def dot_t(a, b):
    return lax.dot_general(a, b, (((1,), (1,)), ((), ())), preferred_element_type=F32)


def add(block, *others):
    out = block.astype(F32)
    for other in others:
        out = out + other.astype(F32)
    return out.astype(BF16)


def swap(block, axis, bits):
    size = lax.axis_size(axis)
    return lax.ppermute(block, axis, [(i, i ^ bits) for i in range(size)])


def hop(block, step, sources):
    return lax.ppermute(block, "tensor", [(i, i + step) for i in sources])


def bits_of(number):
    return [1 << b for b in range(number.bit_length()) if number >> b & 1]


def far(offset):
    return len(bits_of(offset >> 1)) > 1


def line_gather(block, count, direct):
    ups, downs = [], []
    for back in range(1, count):
        if back <= direct:
            ups.append(hop(block, back, range(count - back)))
            downs.append(hop(block, -back, range(back, count)))
        else:
            ups.append(hop(ups[-1], 1, range(back - 1, count - 1)))
            downs.append(hop(downs[-1], -1, range(1, count - back + 1)))
    return ups, downs


def line_scatter(part, count):
    up = down = None
    got = []
    for back in range(count - 1, 0, -1):
        first, second = part[count - back], part[back]
        if up is not None:
            first, second = add(first, up), add(second, down)
            up = down = None
        if back < 3:
            got.append(hop(first, back, range(count - back)))
            got.append(hop(second, -back, range(back, count)))
        else:
            up = hop(first, 1, range(count - back))
            down = hop(second, -1, range(back, count))
    return add(part[0], *got)


def with_partner(held):
    return {**held, **{o + 1: swap(b, "expert", 1) for o, b in held.items()}}


def far_blocks(near, block, size):
    half = block.shape[1] // 2
    held = {0: block, **near}
    for offset in range(2, size, 2):
        if offset not in held:
            low, high = bits_of(offset)[0], bits_of(offset)[-1]
            held[offset] = jnp.concatenate(
                [
                    swap(held[offset ^ low][:, :half], "expert", low),
                    swap(held[offset ^ high][:, half:], "expert", high),
                ],
                axis=1,
            )
    return {o: b for o, b in held.items() if far(o)}


def in_order(held, me):
    rows, columns = held[0].shape
    out = jnp.zeros((rows * len(held), columns), held[0].dtype)
    for offset, block in held.items():
        out = lax.dynamic_update_slice(out, block, ((me ^ offset) * rows, 0))
    return out


def tiles_of(width):
    for tile in (512, 256, LANES):
        if width % tile == 0:
            return width // tile
    return 1


def each(count, step):
    @pl.loop(0, count)
    def _(n):
        step(n)


def cut(n, tile):
    return pl.ds(pl.multiple_of(n * tile, tile), tile)


def stack(refs, x, sem):
    copies, at = [], 0
    for k, ref in enumerate(refs):
        rows = ref.shape[0]
        copies.append(pltpu.make_async_copy(ref, x.at[pl.ds(at, rows), :], sem.at[k]))
        at += rows
    for copy in copies:
        copy.start()

    def wait():
        for copy in copies:
            copy.wait()

    return wait


def columns_in(source, target, tiles, sem):
    tile = target.shape[-1] // tiles

    def copy(n):
        at = cut(n, tile)
        return pltpu.make_async_copy(source.at[:, at], target.at[:, at], sem.at[n])

    each(tiles, lambda n: copy(n).start())
    return lambda n: copy(n).wait()


def rows_out(source, targets, tiles, sem):
    tile = source.shape[-1] // tiles

    def copies(n):
        at, start = cut(n, tile), 0
        for k, target in enumerate(targets):
            rows = target.shape[0]
            yield pltpu.make_async_copy(
                source.at[pl.ds(start, rows), at], target.at[:, at], sem.at[k, n]
            )
            start += rows

    def begin(n):
        for copy in copies(n):
            copy.start()

    def finish(n):
        for copy in copies(n):
            copy.wait()

    return begin, lambda: each(tiles, finish)


def take(refs, *counts):
    out, at = [], 0
    for count in counts:
        out.append(refs[at] if count is None else refs[at:at + count])
        at += 1 if count is None else count
    return out + list(refs[at:])


def pick_kernel(count, lengths, *refs):
    own, ups, downs, slot, outs, group, x, pick, made, sem_in, sem_out, sem_group = take(
        refs, None, count - 1, count - 1, None, len(lengths), None
    )
    place = lax.axis_index("tensor")
    rows = own.shape[0]
    width = x.shape[1]
    tiles = tiles_of(width)

    def into(ref, k):
        return pltpu.make_async_copy(ref, x.at[pl.ds(k * rows, rows), :], sem_in.at[k])

    into(own, 0).start()
    for k in range(1, count):
        @pl.when(place >= k)
        def _():
            into(ups[k - 1], k).start()

        @pl.when(place < k)
        def _():
            into(downs[count - k - 1], k).start()

    places = lax.broadcasted_iota(jnp.int32, pick.shape, 0)
    pick[...] = (places == slot[...]).astype(F32).astype(BF16)
    for k in range(count):
        into(own, k).wait()
    whole = pltpu.make_async_copy(x, group, sem_group)
    whole.start()
    begin, finish = rows_out(made, outs, tiles, sem_out)

    def step(n):
        at = cut(n, width // tiles)
        made[:, at] = dot(pick[...], x[:, at]).astype(BF16)
        begin(n)

    each(tiles, step)
    finish()
    whole.wait()


def expert_kernel(count, *refs):
    blocks, gate_w, up_w, down_w, outs, x, gate, upper, down, hidden, made, *sems = take(
        refs, count, None, None, None, count
    )
    inner, outer = down.shape
    ins, os = tiles_of(inner // 2), tiles_of(outer)
    wait_x = stack(blocks, x, sems[0])
    wait_gate = columns_in(gate_w.at[0], gate, ins, sems[1])
    wait_up = columns_in(up_w.at[0], upper, ins, sems[2])
    wait_down = columns_in(down_w.at[0], down, os, sems[3])
    wait_x()

    def one(n):
        at = cut(n, inner // ins)
        wait_gate(n)
        g = dot(x[...], gate[:, at])
        wait_up(n)
        hidden[:, at] = (jax.nn.silu(g) * dot(x[...], upper[:, at])).astype(BF16)

    each(ins, one)
    begin, finish = rows_out(made, outs, os, sems[4])

    def two(n):
        at = cut(n, outer // os)
        wait_down(n)
        made[:, at] = dot(hidden[...], down[:, at]).astype(BF16)
        begin(n)

    each(os, two)
    finish()


def load_pairs(refs, offsets, start, width, held, sem, core):
    rows = refs[0].shape[0]
    copies = []
    for k, (ref, offset) in enumerate(zip(refs, offsets)):
        at = pl.multiple_of((core ^ (offset & 1)) * rows, rows)
        copies.append(
            pltpu.make_async_copy(
                ref.at[:, pl.ds(start, width)], held.at[k // 2, pl.ds(at, rows), :], sem.at[k]
            )
        )
    for copy in copies:
        copy.start()
    return copies


def columns_of(offset, width):
    pair = lax.axis_index("expert") // 2
    return pl.ds(pl.multiple_of((pair ^ (offset // 2)) * width, LANES), width)


def near_kernel(offsets, inner, *refs):
    group, blocks, out, x, held, made, *sems = take(refs, None, len(offsets))
    core = lax.axis_index("expert") & 1
    whole = pltpu.make_async_copy(group, x, sems[0])
    whole.start()
    copies = load_pairs(blocks, offsets, 0, 2 * inner, held, sems[1], core)
    whole.wait()
    for copy in copies:
        copy.wait()
    pair = held.shape[1]
    tiles = tiles_of(2 * inner)
    begin, finish = rows_out(made, [out], tiles, sems[2])

    def step(n):
        at = cut(n, 2 * inner // tiles)
        total = None
        for k in range(len(offsets) // 2):
            term = dot(x[:, columns_of(offsets[2 * k], pair)], held[k, :, at])
            total = term if total is None else total + term
        made[:, at] = total
        begin(n)

    each(tiles, step)
    finish()


def far_kernel(offsets, late, inner, *refs):
    source, group, blocks, out, x, part, held, down, hidden, made, *sems = take(
        refs, None, None, len(offsets)
    )
    core = lax.axis_index("expert") & 1
    whole = pltpu.make_async_copy(group, x, sems[0])
    whole.start()
    copies = load_pairs(
        [blocks[offsets.index(o)] for o in late], late, 0, 2 * inner, held, sems[1], core
    )
    tiles = tiles_of(inner // 2)
    tile = inner // tiles
    wait_part = columns_in(source, part, 2 * tiles, sems[2])
    later = load_pairs(blocks, offsets, 2 * inner, inner, down, sems[3], core)
    whole.wait()
    for copy in copies:
        copy.wait()
    pair = held.shape[1]

    def step(n):
        sums = []
        for base in (0, tiles):
            at = cut(base + n, tile)
            wait_part(base + n)
            total = part[:, at]
            for k in range(len(late) // 2):
                total = total + dot(x[:, columns_of(late[2 * k], pair)], held[k, :, at])
            sums.append(total)
        hidden[:, cut(n, tile)] = (jax.nn.silu(sums[0]) * sums[1]).astype(BF16)

    each(tiles, step)
    for copy in later:
        copy.wait()
    outs = []
    for k in range(len(offsets) // 2):
        at = columns_of(offsets[2 * k], pair)
        made[:, at] = dot_t(hidden[...], down[k])
        outs.append(pltpu.make_async_copy(made.at[:, at], out.at[:, at], sems[4].at[k]))
        outs[-1].start()
    for copy in outs:
        copy.wait()


def combine_kernel(count, parts, *refs):
    blocks, notes, source, outs, x, shared, made, *sems = take(refs, count, None, None, parts)
    wait_x = stack(blocks, x, sems[0])
    total, width = x.shape
    tiles = tiles_of(width)
    wait_shared = columns_in(source, shared, tiles, sems[1])
    rows = notes.shape[0]
    places = lax.broadcasted_iota(jnp.int32, (rows, total), 1)
    pick = (places == notes[:, 0:1].astype(jnp.int32)).astype(F32).astype(BF16)
    scale = notes[:, 1:2]
    wait_x()
    begin, finish = rows_out(made, outs, tiles, sems[2])

    def step(n):
        at = cut(n, width // tiles)
        routed = dot(pick, x[:, at])
        wait_shared(n)
        made[:, at] = (shared[:, at] + scale * routed).astype(BF16)
        begin(n)

    each(tiles, step)
    finish()


def call(kernel, ins, vmem, outs, scratch, flops, moved):
    return pl.pallas_call(
        kernel,
        out_shape=[jax.ShapeDtypeStruct(shape, kind) for shape, kind in outs],
        in_specs=[VMEM_SPEC if k in vmem else ANY_SPEC for k in range(len(ins))],
        out_specs=[ANY_SPEC] * len(outs),
        scratch_shapes=scratch,
        compiler_params=pltpu.CompilerParams(vmem_limit_bytes=VMEM_BYTES),
        cost_estimate=pl.CostEstimate(flops=flops, bytes_accessed=moved, transcendentals=0),
    )(*ins)


def dma(*shape):
    return pltpu.SemaphoreType.DMA(shape)


def pick_rows(own, ups, downs, slot, lengths):
    count, (rows, width) = len(ups) + 1, own.shape
    group, total = rows * count, sum(lengths)
    tiles = tiles_of(width)
    ins = [own, *ups, *downs, slot[None, :]]
    out = call(
        functools.partial(pick_kernel, count, lengths),
        ins,
        {len(ins) - 1},
        [((length, width), BF16) for length in lengths] + [((group, width), BF16)],
        [
            pltpu.VMEM((group, width), BF16),
            pltpu.VMEM((total, group), BF16),
            pltpu.VMEM((total, width), BF16),
            dma(count),
            dma(len(lengths), tiles),
            pltpu.SemaphoreType.DMA,
        ],
        2 * total * group * width,
        2 * (2 * group + total) * width,
    )
    return out[:-1], out[-1]


def expert_rows(blocks, w_gate, w_up, w_down):
    inner, width = w_down.shape[1:]
    rows = sum(b.shape[0] for b in blocks)
    ins, outs = tiles_of(inner // 2), tiles_of(width)
    return call(
        functools.partial(expert_kernel, len(blocks)),
        [*blocks, w_gate, w_up, w_down],
        (),
        [(b.shape, BF16) for b in blocks],
        [
            pltpu.VMEM((rows, width), BF16),
            pltpu.VMEM((width, inner), BF16),
            pltpu.VMEM((width, inner), BF16),
            pltpu.VMEM((inner, width), BF16),
            pltpu.VMEM((rows, inner), BF16),
            pltpu.VMEM((rows, width), BF16),
            dma(len(blocks)),
            dma(ins),
            dma(ins),
            dma(outs),
            dma(len(blocks), outs),
        ],
        6 * rows * inner * width,
        (4 * rows + 6 * inner) * width,
    )


def shared_near(group, blocks, inner):
    offsets = sorted(blocks)
    rows, (tokens, width) = blocks[0].shape[0], group.shape
    count = len(offsets)
    return call(
        functools.partial(near_kernel, offsets, inner),
        [group, *[blocks[o] for o in offsets]],
        (),
        [((tokens, 2 * inner), F32)],
        [
            pltpu.VMEM((tokens, width), BF16),
            pltpu.VMEM((count // 2, 2 * rows, 2 * inner), BF16),
            pltpu.VMEM((tokens, 2 * inner), F32),
            pltpu.SemaphoreType.DMA,
            dma(count),
            dma(1, tiles_of(2 * inner)),
        ],
        4 * tokens * inner * rows * count,
        4 * rows * inner * count + 8 * tokens * inner,
    )[0]


def shared_far(part, group, blocks, inner):
    offsets = sorted(blocks)
    late = [o for o in offsets if far(o)]
    rows, (tokens, width) = blocks[0].shape[0], group.shape
    count = len(offsets)
    return call(
        functools.partial(far_kernel, offsets, late, inner),
        [part, group, *[blocks[o] for o in offsets]],
        (),
        [((tokens, width), F32)],
        [
            pltpu.VMEM((tokens, width), BF16),
            pltpu.VMEM((tokens, 2 * inner), F32),
            pltpu.VMEM((len(late) // 2, 2 * rows, 2 * inner), BF16),
            pltpu.VMEM((count // 2, 2 * rows, inner), BF16),
            pltpu.VMEM((tokens, inner), BF16),
            pltpu.VMEM((tokens, width), F32),
            pltpu.SemaphoreType.DMA,
            dma(len(late)),
            dma(2 * tiles_of(inner // 2)),
            dma(count),
            dma(count // 2),
        ],
        4 * tokens * inner * rows * len(late) + 2 * tokens * inner * width,
        4 * rows * inner * len(late) + 6 * tokens * width + 8 * tokens * inner,
    )[0]


def combine(blocks, notes, shared, parts):
    group, width = shared.shape
    total = sum(b.shape[0] for b in blocks)
    tiles = tiles_of(width)
    ins = [*blocks, notes, shared]
    return call(
        functools.partial(combine_kernel, len(blocks), parts),
        ins,
        {len(blocks)},
        [((group // parts, width), BF16)] * parts,
        [
            pltpu.VMEM((total, width), BF16),
            pltpu.VMEM((group, width), F32),
            pltpu.VMEM((group, width), BF16),
            dma(len(blocks)),
            dma(tiles),
            dma(parts, tiles),
        ],
        2 * group * total * width,
        (2 * total + 6 * group) * width,
    )


def body(tokens, expert_ids, gates, w_gate, w_up, w_down, s_gate, s_up, s_down):
    size = lax.axis_size("expert")
    count = lax.axis_size("tensor")
    me = lax.axis_index("expert")
    place = lax.axis_index("tensor")
    rows, _ = tokens.shape
    group = rows * count
    experts = w_gate.shape[0] * size
    cap = 2 * group // experts
    half = cap // 2
    inner = s_gate.shape[1]

    ups, downs = line_gather(tokens, count, 2)
    s_all = jnp.concatenate([s_gate, s_up, s_down.T], axis=1)
    near = {bit: swap(s_all, "expert", bit) for bit in bits_of((size - 1) & ~1)}
    notes = jnp.concatenate([expert_ids.astype(F32).T, gates[None, :]], axis=0)
    above, below = line_gather(notes, count, count)
    parts = [notes]
    for back in range(1, count):
        parts.append(jnp.where(place >= back, above[back - 1], below[count - back - 1]))
    notes = jnp.concatenate(parts, axis=1)
    ids, scale = notes[0].astype(jnp.int32), notes[1]

    index = jnp.arange(group, dtype=jnp.int32)
    back = index // rows
    index = jnp.where(back > place, place - back + count, place - back) * rows + index % rows
    same = (ids[:, None] == ids[None, :]) & (index[None, :] < index[:, None])
    spot = jnp.sum(same.astype(jnp.int32), axis=1)
    turned = spot + (place & 1) * half
    turned = jnp.where(turned >= cap, turned - cap, turned)
    base, lengths, total = [], [], 0
    for offset in range(size):
        lengths.append(half if far(offset) else cap)
        base.append(total)
        total += lengths[-1]
    slot = jnp.full((group,), -1, jnp.int32)
    for offset in range(size):
        value = base[offset] + spot
        if far(offset):
            value = jnp.where(turned < half, base[offset] + turned, -1)
        slot = jnp.where(ids ^ me == offset, value, slot)
    slot = lax.optimization_barrier(slot)
    fars = [o for o in range(size) if far(o)]
    nears = [o for o in range(2, size) if not far(o)]

    sent, tokens = pick_rows(tokens, ups, downs, slot, lengths)
    got = {0: sent[0]}
    for o in fars:
        got[o] = swap(sent[o], "expert", o)
    for o in [1] + nears:
        got[o] = swap(sent[o], "expert", o)
    blocks = with_partner({0: s_all, **near})
    part = None
    if 2 * s_all.shape[0] % LANES == 0:
        part = shared_near(tokens, blocks, inner)
    mine = jnp.concatenate([got[o] for o in fars])
    mine, *ready = lax.optimization_barrier((mine, *near.values()))
    near = dict(zip(near, ready))
    other = swap(mine, "tensor", 1)
    blocks = {**blocks, **with_partner(far_blocks(near, s_all, size))}

    home = {}
    home[0], made, mine, theirs = expert_rows([got[0], got[1], mine, other], w_gate, w_up, w_down)
    theirs = swap(theirs, "tensor", 1)
    mine = add(mine, theirs)
    home[1] = swap(made, "expert", 1)
    for k, o in enumerate(fars):
        home[o] = swap(mine[k * half:(k + 1) * half], "expert", o)
    made = expert_rows([got[o] for o in nears], w_gate, w_up, w_down)
    for k, o in enumerate(nears):
        home[o] = swap(made[k], "expert", o)

    if part is not None:
        shared = shared_far(part, tokens, blocks, inner)
    else:
        s_in = in_order({o: b[:, :2 * inner] for o, b in blocks.items()}, me)
        s_out = in_order({o: b[:, 2 * inner:] for o, b in blocks.items()}, me)
        pre = dot(tokens, s_in)
        shared = (jax.nn.silu(pre[:, :inner]) * pre[:, inner:]).astype(BF16)
        shared = dot_t(shared, s_out)

    notes = jnp.stack([slot.astype(F32), scale], axis=1)
    parts = combine([home[o] for o in range(size)], notes, shared, count)
    return line_scatter(parts, count)


def solution(mesh):
    return jax.shard_map(
        body,
        mesh=mesh,
        in_specs=(
            P(("expert", "tensor"), None),
            P(("expert", "tensor"), None),
            P(("expert", "tensor")),
            P("expert", None, "tensor"),
            P("expert", None, "tensor"),
            P("expert", "tensor", None),
            P("expert", "tensor"),
            P("expert", "tensor"),
            P("tensor", "expert"),
        ),
        out_specs=P(("expert", "tensor"), None),
        check_vma=False,
    )
```

```python
import functools

import jax
import jax.numpy as jnp
from jax import lax
from jax.experimental import pallas as pl
from jax.experimental.pallas import tpu as pltpu
from jax.sharding import PartitionSpec as P


F32 = jnp.float32
BF16 = jnp.bfloat16
LANES = 128
PARTS = 2
VMEM_BYTES = 56 * 1024 * 1024
VMEM_SPEC = pl.BlockSpec(memory_space=pltpu.VMEM)
ANY_SPEC = pl.BlockSpec(memory_space=pl.ANY)


def dot(a, b):
    return jnp.dot(a, b, preferred_element_type=F32)


def dot_t(a, b):
    return lax.dot_general(a, b, (((1,), (1,)), ((), ())), preferred_element_type=F32)


def add(block, *others):
    out = block.astype(F32)
    for other in others:
        out = out + other.astype(F32)
    return out.astype(BF16)


def swap(block, axis, bits):
    size = lax.axis_size(axis)
    return lax.ppermute(block, axis, [(i, i ^ bits) for i in range(size)])


def hop(block, step, sources):
    return lax.ppermute(block, "tensor", [(i, i + step) for i in sources])


def bits_of(number):
    return [1 << b for b in range(number.bit_length()) if number >> b & 1]


def far(offset):
    return len(bits_of(offset >> 1)) > 1


def line_all(block, count):
    parts = [block] + [0] * (count - 1)
    for back in range(1, count):
        parts[back] += hop(block, back, range(count - back))
        parts[count - back] += hop(block, -back, range(back, count))
    return parts


def line_gather(block, count):
    if count < 4:
        return {
            k: [(part, range(count))] for k, part in enumerate(line_all(block, count)) if k
        }
    got = {k: [] for k in range(1, count)}
    middle = (count // 2 - 1, count // 2)
    up = hop(block, 2, range(count - 2))
    down = hop(block, -2, range(2, count))
    got[2].append((up, list(range(2, count))))
    got[count - 2].append((down, list(range(count - 2))))
    outer = [i for i in range(count - 1) if i != middle[0]]
    got[1].append((hop(block, 1, outer), [i + 1 for i in outer]))
    outer = [i + 1 for i in outer]
    got[count - 1].append((hop(block, -1, outer), [i - 1 for i in outer]))
    block, up, down = lax.optimization_barrier((block, up, down))
    for back in range(3, count):
        up = hop(up, 1, range(back - 1, count - 1))
        down = hop(down, -1, range(1, count - back + 1))
        got[back].append((up, list(range(back, count))))
        got[count - back].append((down, list(range(count - back))))
    got[1].append((hop(block, 1, middle[:1]), [middle[1]]))
    got[count - 1].append((hop(block, -1, middle[1:]), [middle[0]]))
    return got


def line_scatter(part, count):
    got = []
    for back in range(count - 1, 0, -1):
        got.append(hop(part[count - back], back, range(count - back)))
        got.append(hop(part[back], -back, range(back, count)))
    return add(part[0], *got)


def with_partner(held):
    return {**held, **{o + 1: swap(b, "expert", 1) for o, b in held.items()}}


def far_blocks(near, block, size):
    half = block.shape[1] // 2
    held = {0: block, **near}
    for offset in range(2, size, 2):
        if offset not in held:
            low, high = bits_of(offset)[0], bits_of(offset)[-1]
            pieces = [
                swap(held[offset ^ low][:, :half], "expert", low),
                swap(held[offset ^ high][:, half:], "expert", high),
            ]
            held[offset] = jnp.concatenate(pieces, axis=1)
    return {o: b for o, b in held.items() if far(o)}


def in_order(held, me):
    rows, columns = held[0].shape
    out = jnp.zeros((rows * len(held), columns), held[0].dtype)
    for offset, block in held.items():
        out = lax.dynamic_update_slice(out, block, ((me ^ offset) * rows, 0))
    return out


def tiles_of(width):
    for tile in (512, 256, LANES):
        if width % tile == 0:
            return width // tile
    return 1


def each(count, step):
    @pl.loop(0, count)
    def _(n):
        step(n)


def cut(n, tile):
    return pl.ds(pl.multiple_of(n * tile, tile), tile)


def stack(refs, x, sem):
    copies, at = [], 0
    for k, ref in enumerate(refs):
        rows = ref.shape[0]
        copies.append(pltpu.make_async_copy(ref, x.at[pl.ds(at, rows), :], sem.at[k]))
        at += rows
    for copy in copies:
        copy.start()

    def wait():
        for copy in copies:
            copy.wait()

    return wait


def columns_in(source, target, tiles, sem, base=0):
    tile = target.shape[-1] // tiles

    def copy(n):
        from_at = pl.ds(pl.multiple_of(base + n * tile, LANES), tile)
        return pltpu.make_async_copy(source.at[:, from_at], target.at[:, cut(n, tile)], sem.at[n])

    each(tiles, lambda n: copy(n).start())
    return lambda n: copy(n).wait()


def rows_out(source, targets, tiles, sem, base=0):
    tile = targets[0].shape[-1] // tiles

    def copies(n):
        at, start = pl.ds(pl.multiple_of(base + n * tile, LANES), tile), 0
        for k, target in enumerate(targets):
            rows = target.shape[0]
            yield pltpu.make_async_copy(
                source.at[pl.ds(start, rows), at], target.at[:, cut(n, tile)], sem.at[k, n]
            )
            start += rows

    def begin(n):
        for copy in copies(n):
            copy.start()

    def finish(n):
        for copy in copies(n):
            copy.wait()

    return begin, lambda: each(tiles, finish)


def take(refs, *counts):
    out, at = [], 0
    for count in counts:
        out.append(refs[at] if count is None else refs[at:at + count])
        at += 1 if count is None else count
    return out + list(refs[at:])


def pick_kernel(count, sources, lengths, *refs):
    own, parts, slot, outs, group, x, pick, made, sem_in, sem_out, sem_group = take(
        refs, None, len(sources), None, len(lengths), None
    )
    place = lax.axis_index("tensor")
    rows = own.shape[0]
    width = x.shape[1]
    tiles = tiles_of(width)

    def into(ref, k):
        return pltpu.make_async_copy(ref, x.at[pl.ds(k * rows, rows), :], sem_in.at[k])

    into(own, 0).start()
    for part, (k, places) in zip(parts, sources):
        here = functools.reduce(jnp.logical_or, [place == p for p in places])

        @pl.when(here)
        def _():
            into(part, k).start()

    places = lax.broadcasted_iota(jnp.int32, pick.shape, 0)
    pick[...] = (places == slot[...]).astype(F32).astype(BF16)
    for k in range(count):
        into(own, k).wait()
    whole = pltpu.make_async_copy(x, group, sem_group)
    whole.start()
    begin, finish = rows_out(made, outs, tiles, sem_out)

    def step(n):
        at = cut(n, width // tiles)
        made[:, at] = dot(pick[...], x[:, at]).astype(BF16)
        begin(n)

    each(tiles, step)
    finish()
    whole.wait()


def expert_kernel(count, *refs):
    blocks, gate_w, up_w, down_w, outs, x, gate, upper, down, hidden, made, *sems = take(
        refs, count, None, None, None, PARTS * count
    )
    inner, outer = down.shape
    ins, os = tiles_of(inner // 2), tiles_of(outer // PARTS)
    tile = outer // PARTS // os
    wait_x = stack(blocks, x, sems[0])
    wait_gate = columns_in(gate_w.at[0], gate, ins, sems[1])
    wait_up = columns_in(up_w.at[0], upper, ins, sems[2])
    wait_down = columns_in(down_w.at[0], down, PARTS * os, sems[3])
    wait_x()

    def one(n):
        at = cut(n, inner // ins)
        wait_gate(n)
        g = dot(x[...], gate[:, at])
        wait_up(n)
        hidden[:, at] = (jax.nn.silu(g) * dot(x[...], upper[:, at])).astype(BF16)

    each(ins, one)
    finishes = []
    for c in range(PARTS):
        begin, finish = rows_out(
            made, outs[c * count:(c + 1) * count], os, sems[4].at[c], c * outer // PARTS
        )
        finishes.append(finish)

        def two(n):
            wait_down(c * os + n)
            at = pl.ds(pl.multiple_of((c * os + n) * tile, LANES), tile)
            made[:, at] = dot(hidden[...], down[:, at]).astype(BF16)
            begin(n)

        each(os, two)
    for finish in finishes:
        finish()


def load_pairs(refs, offsets, start, width, held, sem, core):
    rows = refs[0].shape[0]
    copies = []
    for k, (ref, offset) in enumerate(zip(refs, offsets)):
        at = pl.multiple_of((core ^ (offset & 1)) * rows, rows)
        copies.append(
            pltpu.make_async_copy(
                ref.at[:, pl.ds(start, width)], held.at[k // 2, pl.ds(at, rows), :], sem.at[k]
            )
        )
    for copy in copies:
        copy.start()
    return copies


def columns_of(offset, width):
    pair = lax.axis_index("expert") // 2
    return pl.ds(pl.multiple_of((pair ^ (offset // 2)) * width, LANES), width)


def near_kernel(offsets, inner, *refs):
    group, blocks, out, x, held, made, *sems = take(refs, None, len(offsets))
    core = lax.axis_index("expert") & 1
    whole = pltpu.make_async_copy(group, x, sems[0])
    whole.start()
    copies = load_pairs(blocks, offsets, 0, 2 * inner, held, sems[1], core)
    whole.wait()
    for copy in copies:
        copy.wait()
    pair = held.shape[1]
    tiles = tiles_of(2 * inner)
    begin, finish = rows_out(made, [out], tiles, sems[2])

    def step(n):
        at = cut(n, 2 * inner // tiles)
        total = None
        for k in range(len(offsets) // 2):
            term = dot(x[:, columns_of(offsets[2 * k], pair)], held[k, :, at])
            total = term if total is None else total + term
        made[:, at] = total
        begin(n)

    each(tiles, step)
    finish()


def far_kernel(offsets, late, inner, *refs):
    source, group, blocks, out, x, part, held, down, hidden, made, *sems = take(
        refs, None, None, len(offsets)
    )
    core = lax.axis_index("expert") & 1
    whole = pltpu.make_async_copy(group, x, sems[0])
    whole.start()
    copies = load_pairs(
        [blocks[offsets.index(o)] for o in late], late, 0, 2 * inner, held, sems[1], core
    )
    tiles = tiles_of(inner // 2)
    tile = inner // tiles
    wait_part = columns_in(source, part, 2 * tiles, sems[2])
    later = load_pairs(blocks, offsets, 2 * inner, inner, down, sems[3], core)
    whole.wait()
    for copy in copies:
        copy.wait()
    pair = held.shape[1]

    def step(n):
        sums = []
        for base in (0, tiles):
            at = cut(base + n, tile)
            wait_part(base + n)
            total = part[:, at]
            for k in range(len(late) // 2):
                total = total + dot(x[:, columns_of(late[2 * k], pair)], held[k, :, at])
            sums.append(total)
        hidden[:, cut(n, tile)] = (jax.nn.silu(sums[0]) * sums[1]).astype(BF16)

    each(tiles, step)
    for copy in later:
        copy.wait()
    outs = []
    for k in range(len(offsets) // 2):
        at = columns_of(offsets[2 * k], pair)
        made[:, at] = dot_t(hidden[...], down[k])
        outs.append(pltpu.make_async_copy(made.at[:, at], out.at[:, at], sems[4].at[k]))
        outs[-1].start()
    for copy in outs:
        copy.wait()


def combine_kernel(count, parts, base, *refs):
    blocks, notes, source, outs, x, shared, made, *sems = take(refs, count, None, None, parts)
    wait_x = stack(blocks, x, sems[0])
    total, width = x.shape
    tiles = tiles_of(width)
    wait_shared = columns_in(source, shared, tiles, sems[1], base)
    rows = notes.shape[0]
    places = lax.broadcasted_iota(jnp.int32, (rows, total), 1)
    pick = (places == notes[:, 0:1].astype(jnp.int32)).astype(F32).astype(BF16)
    scale = notes[:, 1:2]
    wait_x()
    begin, finish = rows_out(made, outs, tiles, sems[2])

    def step(n):
        at = cut(n, width // tiles)
        routed = dot(pick, x[:, at])
        wait_shared(n)
        made[:, at] = (shared[:, at] + scale * routed).astype(BF16)
        begin(n)

    each(tiles, step)
    finish()


def call(kernel, ins, vmem, outs, scratch, flops, moved):
    return pl.pallas_call(
        kernel,
        out_shape=[jax.ShapeDtypeStruct(shape, kind) for shape, kind in outs],
        in_specs=[VMEM_SPEC if k in vmem else ANY_SPEC for k in range(len(ins))],
        out_specs=[ANY_SPEC] * len(outs),
        scratch_shapes=scratch,
        compiler_params=pltpu.CompilerParams(vmem_limit_bytes=VMEM_BYTES),
        cost_estimate=pl.CostEstimate(flops=flops, bytes_accessed=moved, transcendentals=0),
    )(*ins)


def dma(*shape):
    return pltpu.SemaphoreType.DMA(shape)


def pick_rows(own, got, slot, lengths):
    sources = [(k, places) for k in got for _, places in got[k]]
    count, (rows, width) = len(got) + 1, own.shape
    group, total = rows * count, sum(lengths)
    tiles = tiles_of(width)
    ins = [own, *[block for k in got for block, _ in got[k]], slot[None, :]]
    out = call(
        functools.partial(pick_kernel, count, sources, lengths),
        ins,
        {len(ins) - 1},
        [((length, width), BF16) for length in lengths] + [((group, width), BF16)],
        [
            pltpu.VMEM((group, width), BF16),
            pltpu.VMEM((total, group), BF16),
            pltpu.VMEM((total, width), BF16),
            dma(count),
            dma(len(lengths), tiles),
            pltpu.SemaphoreType.DMA,
        ],
        2 * total * group * width,
        2 * (2 * group + total) * width,
    )
    return out[:-1], out[-1]


def expert_rows(blocks, w_gate, w_up, w_down):
    inner, width = w_down.shape[1:]
    rows, count = sum(b.shape[0] for b in blocks), len(blocks)
    ins, outs = tiles_of(inner // 2), tiles_of(width // PARTS)
    made = call(
        functools.partial(expert_kernel, count),
        [*blocks, w_gate, w_up, w_down],
        (),
        [((b.shape[0], width // PARTS), BF16) for b in blocks] * PARTS,
        [
            pltpu.VMEM((rows, width), BF16),
            pltpu.VMEM((width, inner), BF16),
            pltpu.VMEM((width, inner), BF16),
            pltpu.VMEM((inner, width), BF16),
            pltpu.VMEM((rows, inner), BF16),
            pltpu.VMEM((rows, width), BF16),
            dma(count),
            dma(ins),
            dma(ins),
            dma(PARTS * outs),
            dma(PARTS, count, outs),
        ],
        6 * rows * inner * width,
        (4 * rows + 6 * inner) * width,
    )
    return [made[c * count:(c + 1) * count] for c in range(PARTS)]


def shared_near(group, blocks, inner):
    offsets = sorted(blocks)
    rows, (tokens, width) = blocks[0].shape[0], group.shape
    count = len(offsets)
    return call(
        functools.partial(near_kernel, offsets, inner),
        [group, *[blocks[o] for o in offsets]],
        (),
        [((tokens, 2 * inner), F32)],
        [
            pltpu.VMEM((tokens, width), BF16),
            pltpu.VMEM((count // 2, 2 * rows, 2 * inner), BF16),
            pltpu.VMEM((tokens, 2 * inner), F32),
            pltpu.SemaphoreType.DMA,
            dma(count),
            dma(1, tiles_of(2 * inner)),
        ],
        4 * tokens * inner * rows * count,
        4 * rows * inner * count + 8 * tokens * inner,
    )[0]


def shared_far(part, group, blocks, inner):
    offsets = sorted(blocks)
    late = [o for o in offsets if far(o)]
    rows, (tokens, width) = blocks[0].shape[0], group.shape
    count = len(offsets)
    return call(
        functools.partial(far_kernel, offsets, late, inner),
        [part, group, *[blocks[o] for o in offsets]],
        (),
        [((tokens, width), F32)],
        [
            pltpu.VMEM((tokens, width), BF16),
            pltpu.VMEM((tokens, 2 * inner), F32),
            pltpu.VMEM((len(late) // 2, 2 * rows, 2 * inner), BF16),
            pltpu.VMEM((count // 2, 2 * rows, inner), BF16),
            pltpu.VMEM((tokens, inner), BF16),
            pltpu.VMEM((tokens, width), F32),
            pltpu.SemaphoreType.DMA,
            dma(len(late)),
            dma(2 * tiles_of(inner // 2)),
            dma(count),
            dma(count // 2),
        ],
        4 * tokens * inner * rows * len(late) + 2 * tokens * inner * width,
        4 * rows * inner * len(late) + 6 * tokens * width + 8 * tokens * inner,
    )[0]


def combine(blocks, notes, shared, parts, base):
    group, width = shared.shape[0], blocks[0].shape[1]
    total = sum(b.shape[0] for b in blocks)
    tiles = tiles_of(width)
    ins = [*blocks, notes, shared]
    return call(
        functools.partial(combine_kernel, len(blocks), parts, base),
        ins,
        {len(blocks)},
        [((group // parts, width), BF16)] * parts,
        [
            pltpu.VMEM((total, width), BF16),
            pltpu.VMEM((group, width), F32),
            pltpu.VMEM((group, width), BF16),
            dma(len(blocks)),
            dma(tiles),
            dma(parts, tiles),
        ],
        2 * group * total * width,
        (2 * total + 6 * group) * width,
    )


def body(tokens, expert_ids, gates, w_gate, w_up, w_down, s_gate, s_up, s_down):
    size = lax.axis_size("expert")
    count = lax.axis_size("tensor")
    me = lax.axis_index("expert")
    place = lax.axis_index("tensor")
    rows, width = tokens.shape
    group = rows * count
    experts = w_gate.shape[0] * size
    cap = 2 * group // experts
    half = cap // 2
    inner = s_gate.shape[1]

    gathered = line_gather(tokens, count)
    s_all = jnp.concatenate([s_gate, s_up, s_down.T], axis=1)
    near = {bit: swap(s_all, "expert", bit) for bit in bits_of((size - 1) & ~1)}
    notes = jnp.concatenate([expert_ids.astype(F32).T, gates[None, :]], axis=0)
    notes = jnp.concatenate(line_all(notes, count), axis=1)
    ids, scale = notes[0].astype(jnp.int32), notes[1]

    index = jnp.arange(group, dtype=jnp.int32)
    back = index // rows
    index = jnp.where(back > place, place - back + count, place - back) * rows + index % rows
    same = (ids[:, None] == ids[None, :]) & (index[None, :] < index[:, None])
    spot = jnp.sum(same.astype(jnp.int32), axis=1)
    turned = spot + (place & 1) * half
    turned = jnp.where(turned >= cap, turned - cap, turned)
    base, lengths, total = [], [], 0
    for offset in range(size):
        lengths.append(half if far(offset) else cap)
        base.append(total)
        total += lengths[-1]
    slot = jnp.full((group,), -1, jnp.int32)
    for offset in range(size):
        value = base[offset] + spot
        if far(offset):
            value = jnp.where(turned < half, base[offset] + turned, -1)
        slot = jnp.where(ids ^ me == offset, value, slot)
    slot = lax.optimization_barrier(slot)
    fars = [o for o in range(size) if far(o)]
    nears = [o for o in range(2, size) if not far(o)]

    sent, tokens = pick_rows(tokens, gathered, slot, lengths)
    got = {0: sent[0]}
    for o in fars:
        got[o] = swap(sent[o], "expert", o)
    for o in nears:
        got[o] = swap(sent[o], "expert", o)
    got[1] = swap(sent[1], "expert", 1)
    blocks = with_partner({0: s_all, **near})
    part = None
    if 2 * s_all.shape[0] % LANES == 0:
        part = shared_near(tokens, blocks, inner)
    own = expert_rows([got[0], got[1]], w_gate, w_up, w_down)
    home = [{0: own[c][0]} for c in range(PARTS)]
    for c in range(PARTS):
        home[c][1] = swap(own[c][1], "expert", 1)
    mine = jnp.concatenate([got[o] for o in fars])
    mine, *ready = lax.optimization_barrier((mine, *near.values()))
    near = dict(zip(near, ready))
    other = swap(mine, "tensor", 1)
    late = far_blocks(near, s_all, size)
    made = expert_rows([mine, other], w_gate, w_up, w_down)
    pair = []
    for c in range(PARTS):
        pair.append((made[c][0], swap(made[c][1], "tensor", 1)))
    made = expert_rows([got[o] for o in nears], w_gate, w_up, w_down)
    for c in range(PARTS):
        mine = add(*pair[c])
        for k, o in enumerate(fars):
            home[c][o] = swap(mine[k * half:(k + 1) * half], "expert", o)
        for k, o in enumerate(nears):
            home[c][o] = swap(made[c][k], "expert", o)
    blocks = {**blocks, **with_partner(late)}

    if part is not None:
        shared = shared_far(part, tokens, blocks, inner)
    else:
        s_in = in_order({o: b[:, :2 * inner] for o, b in blocks.items()}, me)
        s_out = in_order({o: b[:, 2 * inner:] for o, b in blocks.items()}, me)
        pre = dot(tokens, s_in)
        shared = (jax.nn.silu(pre[:, :inner]) * pre[:, inner:]).astype(BF16)
        shared = dot_t(shared, s_out)

    notes = jnp.stack([slot.astype(F32), scale], axis=1)
    outs = []
    for c in range(PARTS):
        parts = combine([home[c][o] for o in range(size)], notes, shared, count, c * width // PARTS)
        outs.append(line_scatter(parts, count))
    return jnp.concatenate(outs, axis=1)


def solution(mesh):
    return jax.shard_map(
        body,
        mesh=mesh,
        in_specs=(
            P(("expert", "tensor"), None),
            P(("expert", "tensor"), None),
            P(("expert", "tensor")),
            P("expert", None, "tensor"),
            P("expert", None, "tensor"),
            P("expert", "tensor", None),
            P("expert", "tensor"),
            P("expert", "tensor"),
            P("tensor", "expert"),
        ),
        out_specs=P(("expert", "tensor"), None),
        check_vma=False,
    )
```

```python
import functools

import jax
import jax.numpy as jnp
from jax import lax
from jax.experimental import pallas as pl
from jax.experimental.pallas import tpu as pltpu
from jax.sharding import PartitionSpec as P


F32 = jnp.float32
BF16 = jnp.bfloat16
LANES = 128
PARTS = 2
VMEM_BYTES = 56 * 1024 * 1024
VMEM_SPEC = pl.BlockSpec(memory_space=pltpu.VMEM)
ANY_SPEC = pl.BlockSpec(memory_space=pl.ANY)


def dot(a, b):
    return jnp.dot(a, b, preferred_element_type=F32)


def dot_t(a, b):
    return lax.dot_general(a, b, (((1,), (1,)), ((), ())), preferred_element_type=F32)


def add(block, *others):
    out = block.astype(F32)
    for other in others:
        out = out + other.astype(F32)
    return out.astype(BF16)


def swap(block, axis, bits):
    size = lax.axis_size(axis)
    return lax.ppermute(block, axis, [(i, i ^ bits) for i in range(size)])


def ring(block, step):
    count = lax.axis_size("tensor")
    return lax.ppermute(block, "tensor", [(i, (i + step) % count) for i in range(count)])


def bits_of(number):
    return [1 << b for b in range(number.bit_length()) if number >> b & 1]


def far(offset):
    return len(bits_of(offset >> 1)) > 1


def line_gather(block, count):
    if count != 4:
        return [(ring(block, back), [(back, range(count))]) for back in range(1, count)]
    direct = ring(block, 2)
    outer = swap(block, "tensor", 1)
    block, direct = lax.optimization_barrier((block, direct))
    ahead = lax.ppermute(direct, "tensor", [(2, 3), (1, 0)])
    middle = lax.ppermute(block, "tensor", [(1, 2), (2, 1)])
    return [
        (direct, [(2, range(4))]),
        (outer, [(1, (1, 3)), (3, (0, 2))]),
        (ahead, [(1, (0,)), (3, (3,))]),
        (middle, [(1, (2,)), (3, (1,))]),
    ]


def line_scatter(part, count):
    return add(part[0], *[ring(part[k], -k) for k in range(1, count)])


def with_partner(held):
    return {**held, **{o + 1: swap(b, "expert", 1) for o, b in held.items()}}


def far_blocks(near, block, size):
    half = block.shape[1] // 2
    held = {0: block, **near}
    for offset in range(2, size, 2):
        if offset not in held:
            low, high = bits_of(offset)[0], bits_of(offset)[-1]
            pieces = [
                swap(held[offset ^ low][:, :half], "expert", low),
                swap(held[offset ^ high][:, half:], "expert", high),
            ]
            held[offset] = jnp.concatenate(pieces, axis=1)
    return {o: b for o, b in held.items() if far(o)}


def in_order(held, me):
    rows, columns = held[0].shape
    out = jnp.zeros((rows * len(held), columns), held[0].dtype)
    for offset, block in held.items():
        out = lax.dynamic_update_slice(out, block, ((me ^ offset) * rows, 0))
    return out


def tiles_of(width):
    for tile in (512, 256, LANES):
        if width % tile == 0:
            return width // tile
    return 1


def each(count, step):
    @pl.loop(0, count)
    def _(n):
        step(n)


def cut(n, tile):
    return pl.ds(pl.multiple_of(n * tile, tile), tile)


def stack(refs, x, sem):
    copies, at = [], 0
    for k, ref in enumerate(refs):
        rows = ref.shape[0]
        copies.append(pltpu.make_async_copy(ref, x.at[pl.ds(at, rows), :], sem.at[k]))
        at += rows
    for copy in copies:
        copy.start()

    def wait():
        for copy in copies:
            copy.wait()

    return wait


def columns_in(source, target, tiles, sem, base=0):
    tile = target.shape[-1] // tiles

    def copy(n):
        from_at = pl.ds(pl.multiple_of(base + n * tile, LANES), tile)
        return pltpu.make_async_copy(source.at[:, from_at], target.at[:, cut(n, tile)], sem.at[n])

    each(tiles, lambda n: copy(n).start())
    return lambda n: copy(n).wait()


def rows_out(source, targets, tiles, sem, base=0):
    tile = targets[0].shape[-1] // tiles

    def copies(n):
        at, start = pl.ds(pl.multiple_of(base + n * tile, LANES), tile), 0
        for k, target in enumerate(targets):
            rows = target.shape[0]
            yield pltpu.make_async_copy(
                source.at[pl.ds(start, rows), at], target.at[:, cut(n, tile)], sem.at[k, n]
            )
            start += rows

    def begin(n):
        for copy in copies(n):
            copy.start()

    def finish(n):
        for copy in copies(n):
            copy.wait()

    return begin, lambda: each(tiles, finish)


def take(refs, *counts):
    out, at = [], 0
    for count in counts:
        out.append(refs[at] if count is None else refs[at:at + count])
        at += 1 if count is None else count
    return out + list(refs[at:])


def pick_kernel(count, sources, lengths, *refs):
    own, parts, slot, outs, group, x, pick, made, sem_in, sem_out, sem_group = take(
        refs, None, len(sources), None, len(lengths), None
    )
    place = lax.axis_index("tensor")
    rows = own.shape[0]
    width = x.shape[1]
    tiles = tiles_of(width)

    def into(ref, k):
        return pltpu.make_async_copy(ref, x.at[pl.ds(k * rows, rows), :], sem_in.at[k])

    into(own, 0).start()
    for part, uses in zip(parts, sources):
        for k, places in uses:
            here = functools.reduce(jnp.logical_or, [place == p for p in places])

            @pl.when(here)
            def _():
                into(part, k).start()

    places = lax.broadcasted_iota(jnp.int32, pick.shape, 0)
    pick[...] = (places == slot[...]).astype(F32).astype(BF16)
    for k in range(count):
        into(own, k).wait()
    whole = pltpu.make_async_copy(x, group, sem_group)
    whole.start()
    begin, finish = rows_out(made, outs, tiles, sem_out)

    def step(n):
        at = cut(n, width // tiles)
        made[:, at] = dot(pick[...], x[:, at]).astype(BF16)
        begin(n)

    each(tiles, step)
    finish()
    whole.wait()


def expert_kernel(count, *refs):
    blocks, gate_w, up_w, down_w, outs, x, gate, upper, down, hidden, made, *sems = take(
        refs, count, None, None, None, PARTS * count
    )
    inner, outer = down.shape
    ins, os = tiles_of(inner // 2), tiles_of(outer // PARTS)
    tile = outer // PARTS // os
    wait_x = stack(blocks, x, sems[0])
    wait_gate = columns_in(gate_w.at[0], gate, ins, sems[1])
    wait_up = columns_in(up_w.at[0], upper, ins, sems[2])
    wait_down = columns_in(down_w.at[0], down, PARTS * os, sems[3])
    wait_x()

    def one(n):
        at = cut(n, inner // ins)
        wait_gate(n)
        g = dot(x[...], gate[:, at])
        wait_up(n)
        hidden[:, at] = (jax.nn.silu(g) * dot(x[...], upper[:, at])).astype(BF16)

    each(ins, one)
    finishes = []
    for c in range(PARTS):
        begin, finish = rows_out(
            made, outs[c * count:(c + 1) * count], os, sems[4].at[c], c * outer // PARTS
        )
        finishes.append(finish)

        def two(n):
            wait_down(c * os + n)
            at = pl.ds(pl.multiple_of((c * os + n) * tile, LANES), tile)
            made[:, at] = dot(hidden[...], down[:, at]).astype(BF16)
            begin(n)

        each(os, two)
    for finish in finishes:
        finish()


def load_pairs(refs, offsets, start, width, held, sem, core):
    rows = refs[0].shape[0]
    copies = []
    for k, (ref, offset) in enumerate(zip(refs, offsets)):
        at = pl.multiple_of((core ^ (offset & 1)) * rows, rows)
        copies.append(
            pltpu.make_async_copy(
                ref.at[:, pl.ds(start, width)], held.at[k // 2, pl.ds(at, rows), :], sem.at[k]
            )
        )
    for copy in copies:
        copy.start()
    return copies


def columns_of(offset, width):
    pair = lax.axis_index("expert") // 2
    return pl.ds(pl.multiple_of((pair ^ (offset // 2)) * width, LANES), width)


def near_kernel(offsets, inner, *refs):
    group, blocks, out, x, held, made, *sems = take(refs, None, len(offsets))
    core = lax.axis_index("expert") & 1
    whole = pltpu.make_async_copy(group, x, sems[0])
    whole.start()
    copies = load_pairs(blocks, offsets, 0, 2 * inner, held, sems[1], core)
    whole.wait()
    for copy in copies:
        copy.wait()
    pair = held.shape[1]
    tiles = tiles_of(2 * inner)
    begin, finish = rows_out(made, [out], tiles, sems[2])

    def step(n):
        at = cut(n, 2 * inner // tiles)
        total = None
        for k in range(len(offsets) // 2):
            term = dot(x[:, columns_of(offsets[2 * k], pair)], held[k, :, at])
            total = term if total is None else total + term
        made[:, at] = total
        begin(n)

    each(tiles, step)
    finish()


def far_kernel(offsets, late, inner, *refs):
    source, group, blocks, out, x, part, held, down, hidden, made, *sems = take(
        refs, None, None, len(offsets)
    )
    core = lax.axis_index("expert") & 1
    whole = pltpu.make_async_copy(group, x, sems[0])
    whole.start()
    copies = load_pairs(
        [blocks[offsets.index(o)] for o in late], late, 0, 2 * inner, held, sems[1], core
    )
    tiles = tiles_of(inner // 2)
    tile = inner // tiles
    wait_part = columns_in(source, part, 2 * tiles, sems[2])
    later = load_pairs(blocks, offsets, 2 * inner, inner, down, sems[3], core)
    whole.wait()
    for copy in copies:
        copy.wait()
    pair = held.shape[1]

    def step(n):
        sums = []
        for base in (0, tiles):
            at = cut(base + n, tile)
            wait_part(base + n)
            total = part[:, at]
            for k in range(len(late) // 2):
                total = total + dot(x[:, columns_of(late[2 * k], pair)], held[k, :, at])
            sums.append(total)
        hidden[:, cut(n, tile)] = (jax.nn.silu(sums[0]) * sums[1]).astype(BF16)

    each(tiles, step)
    for copy in later:
        copy.wait()
    outs = []
    for k in range(len(offsets) // 2):
        at = columns_of(offsets[2 * k], pair)
        made[:, at] = dot_t(hidden[...], down[k])
        outs.append(pltpu.make_async_copy(made.at[:, at], out.at[:, at], sems[4].at[k]))
        outs[-1].start()
    for copy in outs:
        copy.wait()


def combine_kernel(count, parts, base, *refs):
    blocks, notes, source, outs, x, shared, made, *sems = take(refs, count, None, None, parts)
    wait_x = stack(blocks, x, sems[0])
    total, width = x.shape
    tiles = tiles_of(width)
    wait_shared = columns_in(source, shared, tiles, sems[1], base)
    rows = notes.shape[0]
    places = lax.broadcasted_iota(jnp.int32, (rows, total), 1)
    pick = (places == notes[:, 0:1].astype(jnp.int32)).astype(F32).astype(BF16)
    scale = notes[:, 1:2]
    wait_x()
    begin, finish = rows_out(made, outs, tiles, sems[2])

    def step(n):
        at = cut(n, width // tiles)
        routed = dot(pick, x[:, at])
        wait_shared(n)
        made[:, at] = (shared[:, at] + scale * routed).astype(BF16)
        begin(n)

    each(tiles, step)
    finish()


def call(kernel, ins, vmem, outs, scratch, flops, moved):
    return pl.pallas_call(
        kernel,
        out_shape=[jax.ShapeDtypeStruct(shape, kind) for shape, kind in outs],
        in_specs=[VMEM_SPEC if k in vmem else ANY_SPEC for k in range(len(ins))],
        out_specs=[ANY_SPEC] * len(outs),
        scratch_shapes=scratch,
        compiler_params=pltpu.CompilerParams(vmem_limit_bytes=VMEM_BYTES),
        cost_estimate=pl.CostEstimate(flops=flops, bytes_accessed=moved, transcendentals=0),
    )(*ins)


def dma(*shape):
    return pltpu.SemaphoreType.DMA(shape)


def pick_rows(own, got, slot, lengths):
    sources = [uses for _, uses in got]
    count, (rows, width) = lax.axis_size("tensor"), own.shape
    group, total = rows * count, sum(lengths)
    tiles = tiles_of(width)
    ins = [own, *[block for block, _ in got], slot[None, :]]
    out = call(
        functools.partial(pick_kernel, count, sources, lengths),
        ins,
        {len(ins) - 1},
        [((length, width), BF16) for length in lengths] + [((group, width), BF16)],
        [
            pltpu.VMEM((group, width), BF16),
            pltpu.VMEM((total, group), BF16),
            pltpu.VMEM((total, width), BF16),
            dma(count),
            dma(len(lengths), tiles),
            pltpu.SemaphoreType.DMA,
        ],
        2 * total * group * width,
        2 * (2 * group + total) * width,
    )
    return out[:-1], out[-1]


def expert_rows(blocks, w_gate, w_up, w_down):
    inner, width = w_down.shape[1:]
    rows, count = sum(b.shape[0] for b in blocks), len(blocks)
    ins, outs = tiles_of(inner // 2), tiles_of(width // PARTS)
    made = call(
        functools.partial(expert_kernel, count),
        [*blocks, w_gate, w_up, w_down],
        (),
        [((b.shape[0], width // PARTS), BF16) for b in blocks] * PARTS,
        [
            pltpu.VMEM((rows, width), BF16),
            pltpu.VMEM((width, inner), BF16),
            pltpu.VMEM((width, inner), BF16),
            pltpu.VMEM((inner, width), BF16),
            pltpu.VMEM((rows, inner), BF16),
            pltpu.VMEM((rows, width), BF16),
            dma(count),
            dma(ins),
            dma(ins),
            dma(PARTS * outs),
            dma(PARTS, count, outs),
        ],
        6 * rows * inner * width,
        (4 * rows + 6 * inner) * width,
    )
    return [made[c * count:(c + 1) * count] for c in range(PARTS)]


def shared_near(group, blocks, inner):
    offsets = sorted(blocks)
    rows, (tokens, width) = blocks[0].shape[0], group.shape
    count = len(offsets)
    return call(
        functools.partial(near_kernel, offsets, inner),
        [group, *[blocks[o] for o in offsets]],
        (),
        [((tokens, 2 * inner), F32)],
        [
            pltpu.VMEM((tokens, width), BF16),
            pltpu.VMEM((count // 2, 2 * rows, 2 * inner), BF16),
            pltpu.VMEM((tokens, 2 * inner), F32),
            pltpu.SemaphoreType.DMA,
            dma(count),
            dma(1, tiles_of(2 * inner)),
        ],
        4 * tokens * inner * rows * count,
        4 * rows * inner * count + 8 * tokens * inner,
    )[0]


def shared_far(part, group, blocks, inner):
    offsets = sorted(blocks)
    late = [o for o in offsets if far(o)]
    rows, (tokens, width) = blocks[0].shape[0], group.shape
    count = len(offsets)
    return call(
        functools.partial(far_kernel, offsets, late, inner),
        [part, group, *[blocks[o] for o in offsets]],
        (),
        [((tokens, width), F32)],
        [
            pltpu.VMEM((tokens, width), BF16),
            pltpu.VMEM((tokens, 2 * inner), F32),
            pltpu.VMEM((len(late) // 2, 2 * rows, 2 * inner), BF16),
            pltpu.VMEM((count // 2, 2 * rows, inner), BF16),
            pltpu.VMEM((tokens, inner), BF16),
            pltpu.VMEM((tokens, width), F32),
            pltpu.SemaphoreType.DMA,
            dma(len(late)),
            dma(2 * tiles_of(inner // 2)),
            dma(count),
            dma(count // 2),
        ],
        4 * tokens * inner * rows * len(late) + 2 * tokens * inner * width,
        4 * rows * inner * len(late) + 6 * tokens * width + 8 * tokens * inner,
    )[0]


def combine(blocks, notes, shared, parts, base):
    group, width = shared.shape[0], blocks[0].shape[1]
    total = sum(b.shape[0] for b in blocks)
    tiles = tiles_of(width)
    ins = [*blocks, notes, shared]
    return call(
        functools.partial(combine_kernel, len(blocks), parts, base),
        ins,
        {len(blocks)},
        [((group // parts, width), BF16)] * parts,
        [
            pltpu.VMEM((total, width), BF16),
            pltpu.VMEM((group, width), F32),
            pltpu.VMEM((group, width), BF16),
            dma(len(blocks)),
            dma(tiles),
            dma(parts, tiles),
        ],
        2 * group * total * width,
        (2 * total + 6 * group) * width,
    )


def body(tokens, expert_ids, gates, w_gate, w_up, w_down, s_gate, s_up, s_down):
    size = lax.axis_size("expert")
    count = lax.axis_size("tensor")
    me = lax.axis_index("expert")
    place = lax.axis_index("tensor")
    rows, width = tokens.shape
    group = rows * count
    experts = w_gate.shape[0] * size
    cap = 2 * group // experts
    half = cap // 2
    inner = s_gate.shape[1]

    gathered = line_gather(tokens, count)
    s_all = jnp.concatenate([s_gate, s_up, s_down.T], axis=1)
    near = {bit: swap(s_all, "expert", bit) for bit in bits_of((size - 1) & ~1)}
    notes = jnp.concatenate([expert_ids.astype(F32).T, gates[None, :]], axis=0)
    others = [ring(notes, back) for back in range(1, count)]
    notes = jnp.concatenate([notes, *others], axis=1)
    ids, scale = notes[0].astype(jnp.int32), notes[1]

    index = jnp.arange(group, dtype=jnp.int32)
    back = index // rows
    index = jnp.where(back > place, place - back + count, place - back) * rows + index % rows
    same = (ids[:, None] == ids[None, :]) & (index[None, :] < index[:, None])
    spot = jnp.sum(same.astype(jnp.int32), axis=1)
    turned = spot + (place & 1) * half
    turned = jnp.where(turned >= cap, turned - cap, turned)
    base, lengths, total = [], [], 0
    for offset in range(size):
        lengths.append(half if far(offset) else cap)
        base.append(total)
        total += lengths[-1]
    slot = jnp.full((group,), -1, jnp.int32)
    for offset in range(size):
        value = base[offset] + spot
        if far(offset):
            value = jnp.where(turned < half, base[offset] + turned, -1)
        slot = jnp.where(ids ^ me == offset, value, slot)
    slot = lax.optimization_barrier(slot)
    fars = [o for o in range(size) if far(o)]
    nears = [o for o in range(2, size) if not far(o)]

    sent, tokens = pick_rows(tokens, gathered, slot, lengths)
    got = {0: sent[0]}
    for o in fars:
        got[o] = swap(sent[o], "expert", o)
    for o in nears:
        got[o] = swap(sent[o], "expert", o)
    got[1] = swap(sent[1], "expert", 1)
    blocks = with_partner({0: s_all, **near})
    part = None
    if 2 * s_all.shape[0] % LANES == 0:
        part = shared_near(tokens, blocks, inner)
    own = expert_rows([got[0], got[1]], w_gate, w_up, w_down)
    home = [{0: own[c][0]} for c in range(PARTS)]
    for c in range(PARTS):
        home[c][1] = swap(own[c][1], "expert", 1)
    mine = jnp.concatenate([got[o] for o in fars])
    mine, *ready = lax.optimization_barrier((mine, *near.values()))
    near = dict(zip(near, ready))
    other = swap(mine, "tensor", 1)
    late = far_blocks(near, s_all, size)
    made = expert_rows([mine, other], w_gate, w_up, w_down)
    pair = []
    for c in range(PARTS):
        pair.append((made[c][0], swap(made[c][1], "tensor", 1)))
    made = expert_rows([got[o] for o in nears], w_gate, w_up, w_down)
    for c in range(PARTS):
        mine = add(*pair[c])
        for k, o in enumerate(fars):
            home[c][o] = swap(mine[k * half:(k + 1) * half], "expert", o)
        for k, o in enumerate(nears):
            home[c][o] = swap(made[c][k], "expert", o)
    blocks = {**blocks, **with_partner(late)}

    if part is not None:
        shared = shared_far(part, tokens, blocks, inner)
    else:
        s_in = in_order({o: b[:, :2 * inner] for o, b in blocks.items()}, me)
        s_out = in_order({o: b[:, 2 * inner:] for o, b in blocks.items()}, me)
        pre = dot(tokens, s_in)
        shared = (jax.nn.silu(pre[:, :inner]) * pre[:, inner:]).astype(BF16)
        shared = dot_t(shared, s_out)

    notes = jnp.stack([slot.astype(F32), scale], axis=1)
    outs = []
    for c in range(PARTS):
        parts = combine([home[c][o] for o in range(size)], notes, shared, count, c * width // PARTS)
        outs.append(line_scatter(parts, count))
    return jnp.concatenate(outs, axis=1)


def solution(mesh):
    return jax.shard_map(
        body,
        mesh=mesh,
        in_specs=(
            P(("expert", "tensor"), None),
            P(("expert", "tensor"), None),
            P(("expert", "tensor")),
            P("expert", None, "tensor"),
            P("expert", None, "tensor"),
            P("expert", "tensor", None),
            P("expert", "tensor"),
            P("expert", "tensor"),
            P("tensor", "expert"),
        ),
        out_specs=P(("expert", "tensor"), None),
        check_vma=False,
    )
```

```python
import functools

import jax
import jax.numpy as jnp
from jax import lax
from jax.experimental import pallas as pl
from jax.experimental.pallas import tpu as pltpu
from jax.sharding import PartitionSpec as P


F32 = jnp.float32
BF16 = jnp.bfloat16
LANES = 128
PARTS = 2
FIRST_PART = 3, 5
VMEM_BYTES = 56 * 1024 * 1024
VMEM_SPEC = pl.BlockSpec(memory_space=pltpu.VMEM)
ANY_SPEC = pl.BlockSpec(memory_space=pl.ANY)


def dot(a, b):
    return jnp.dot(a, b, preferred_element_type=F32)


def dot_t(a, b):
    return lax.dot_general(a, b, (((1,), (1,)), ((), ())), preferred_element_type=F32)


def add(block, *others):
    out = block.astype(F32)
    for other in others:
        out = out + other.astype(F32)
    return out.astype(BF16)


def swap(block, axis, bits):
    size = lax.axis_size(axis)
    return lax.ppermute(block, axis, [(i, i ^ bits) for i in range(size)])


def ring(block, step):
    count = lax.axis_size("tensor")
    return lax.ppermute(block, "tensor", [(i, (i + step) % count) for i in range(count)])


def bits_of(number):
    return [1 << b for b in range(number.bit_length()) if number >> b & 1]


def far(offset):
    return len(bits_of(offset >> 1)) > 1


def line_gather(block, count):
    if count != 4:
        return [(ring(block, back), [(back, range(count))]) for back in range(1, count)]
    direct = ring(block, 2)
    outer = swap(block, "tensor", 1)
    block, direct = lax.optimization_barrier((block, direct))
    ahead = lax.ppermute(direct, "tensor", [(2, 3), (1, 0)])
    middle = lax.ppermute(block, "tensor", [(1, 2), (2, 1)])
    return [
        (direct, [(2, range(4))]),
        (outer, [(1, (1, 3)), (3, (0, 2))]),
        (ahead, [(1, (0,)), (3, (3,))]),
        (middle, [(1, (2,)), (3, (1,))]),
    ]


def line_scatter(part, count):
    return add(part[0], *[ring(part[k], -k) for k in range(1, count)])


def line_scatter_staged(part, place, count):
    if count != 4:
        return line_scatter(part, count)
    odd = (place & 1) > 0
    inward = jnp.where(odd, part[3], part[1])
    ahead = lax.ppermute(inward, "tensor", [(0, 1), (3, 2)])
    middle = lax.ppermute(inward, "tensor", [(1, 2), (2, 1)])
    direct = ring(add(part[2], ahead), 2)
    outer = swap(jnp.where(odd, part[1], part[3]), "tensor", 1)
    return add(part[0], direct, outer, middle)


def with_partner(held):
    return {**held, **{o + 1: swap(b, "expert", 1) for o, b in held.items()}}


def far_blocks(near, block, size):
    half = block.shape[1] // 2
    held = {0: block, **near}
    for offset in range(2, size, 2):
        if offset not in held:
            low, high = bits_of(offset)[0], bits_of(offset)[-1]
            pieces = [
                swap(held[offset ^ low][:, :half], "expert", low),
                swap(held[offset ^ high][:, half:], "expert", high),
            ]
            held[offset] = jnp.concatenate(pieces, axis=1)
    return {o: b for o, b in held.items() if far(o)}


def in_order(held, me):
    rows, columns = held[0].shape
    out = jnp.zeros((rows * len(held), columns), held[0].dtype)
    for offset, block in held.items():
        out = lax.dynamic_update_slice(out, block, ((me ^ offset) * rows, 0))
    return out


def tiles_of(width):
    for tile in (512, 256, LANES):
        if width % tile == 0:
            return width // tile
    return 1


def each(count, step):
    @pl.loop(0, count)
    def _(n):
        step(n)


def cut(n, tile):
    return pl.ds(pl.multiple_of(n * tile, tile), tile)


def stack(refs, x, sem):
    copies, at = [], 0
    for k, ref in enumerate(refs):
        rows = ref.shape[0]
        copies.append(pltpu.make_async_copy(ref, x.at[pl.ds(at, rows), :], sem.at[k]))
        at += rows
    for copy in copies:
        copy.start()

    def wait():
        for copy in copies:
            copy.wait()

    return wait


def columns_in(source, target, tiles, sem, base=0):
    tile = target.shape[-1] // tiles

    def copy(n):
        from_at = pl.ds(pl.multiple_of(base + n * tile, LANES), tile)
        return pltpu.make_async_copy(source.at[:, from_at], target.at[:, cut(n, tile)], sem.at[n])

    each(tiles, lambda n: copy(n).start())
    return lambda n: copy(n).wait()


def rows_out(source, targets, tiles, sem, base=0):
    tile = targets[0].shape[-1] // tiles

    def copies(n):
        at, start = pl.ds(pl.multiple_of(base + n * tile, LANES), tile), 0
        for k, target in enumerate(targets):
            rows = target.shape[0]
            yield pltpu.make_async_copy(
                source.at[pl.ds(start, rows), at], target.at[:, cut(n, tile)], sem.at[k, n]
            )
            start += rows

    def begin(n):
        for copy in copies(n):
            copy.start()

    def finish(n):
        for copy in copies(n):
            copy.wait()

    return begin, lambda: each(tiles, finish)


def column_cuts(width):
    above, below = FIRST_PART
    first = max(LANES, width * above // below // LANES * LANES)
    return [(0, first), (first, width - first)]


def part_tile(width):
    for tile in (512, 256, LANES):
        if all(base % tile == 0 and wide % tile == 0 for base, wide in column_cuts(width)):
            return tile
    raise ValueError(width)


def take(refs, *counts):
    out, at = [], 0
    for count in counts:
        out.append(refs[at] if count is None else refs[at:at + count])
        at += 1 if count is None else count
    return out + list(refs[at:])


def pick_kernel(count, sources, lengths, *refs):
    own, parts, slot, outs, group, x, pick, made, sem_in, sem_out, sem_group = take(
        refs, None, len(sources), None, len(lengths), None
    )
    place = lax.axis_index("tensor")
    rows = own.shape[0]
    width = x.shape[1]
    tiles = tiles_of(width)

    def into(ref, k):
        return pltpu.make_async_copy(ref, x.at[pl.ds(k * rows, rows), :], sem_in.at[k])

    into(own, 0).start()
    for part, uses in zip(parts, sources):
        for k, places in uses:
            here = functools.reduce(jnp.logical_or, [place == p for p in places])

            @pl.when(here)
            def _():
                into(part, k).start()

    places = lax.broadcasted_iota(jnp.int32, pick.shape, 0)
    pick[...] = (places == slot[...]).astype(F32).astype(BF16)
    for k in range(count):
        into(own, k).wait()
    whole = pltpu.make_async_copy(x, group, sem_group)
    whole.start()
    begin, finish = rows_out(made, outs, tiles, sem_out)

    def step(n):
        at = cut(n, width // tiles)
        made[:, at] = dot(pick[...], x[:, at]).astype(BF16)
        begin(n)

    each(tiles, step)
    finish()
    whole.wait()


def expert_kernel(count, *refs):
    blocks, gate_w, up_w, down_w, outs, x, gate, upper, down, hidden, made, *sems = take(
        refs, count, None, None, None, PARTS * count
    )
    inner, outer = down.shape
    ins, tiles = tiles_of(inner // 2), outer // part_tile(outer)
    wait_x = stack(blocks, x, sems[0])
    wait_gate = columns_in(gate_w.at[0], gate, ins, sems[1])
    wait_up = columns_in(up_w.at[0], upper, ins, sems[2])
    wait_down = columns_in(down_w.at[0], down, tiles, sems[3])
    wait_x()

    def one(n):
        at = cut(n, inner // ins)
        wait_gate(n)
        g = dot(x[...], gate[:, at])
        wait_up(n)
        hidden[:, at] = (jax.nn.silu(g) * dot(x[...], upper[:, at])).astype(BF16)

    each(ins, one)
    finishes, tile = [], outer // tiles
    for c, (base, width) in enumerate(column_cuts(outer)):
        begin, finish = rows_out(
            made, outs[c * count:(c + 1) * count], width // tile, sems[4].at[c], base
        )
        finishes.append(finish)

        def two(n):
            wait_down(base // tile + n)
            at = pl.ds(pl.multiple_of(base + n * tile, LANES), tile)
            made[:, at] = dot(hidden[...], down[:, at]).astype(BF16)
            begin(n)

        each(width // tile, two)
    for finish in finishes:
        finish()


def load_pairs(refs, offsets, start, width, held, sem, core):
    rows = refs[0].shape[0]
    copies = []
    for k, (ref, offset) in enumerate(zip(refs, offsets)):
        at = pl.multiple_of((core ^ (offset & 1)) * rows, rows)
        copies.append(
            pltpu.make_async_copy(
                ref.at[:, pl.ds(start, width)], held.at[k // 2, pl.ds(at, rows), :], sem.at[k]
            )
        )
    for copy in copies:
        copy.start()
    return copies


def columns_of(offset, width):
    pair = lax.axis_index("expert") // 2
    return pl.ds(pl.multiple_of((pair ^ (offset // 2)) * width, LANES), width)


def near_kernel(offsets, inner, *refs):
    group, blocks, out, x, held, made, *sems = take(refs, None, len(offsets))
    core = lax.axis_index("expert") & 1
    whole = pltpu.make_async_copy(group, x, sems[0])
    whole.start()
    copies = load_pairs(blocks, offsets, 0, 2 * inner, held, sems[1], core)
    whole.wait()
    for copy in copies:
        copy.wait()
    pair = held.shape[1]
    tiles = tiles_of(2 * inner)
    begin, finish = rows_out(made, [out], tiles, sems[2])

    def step(n):
        at = cut(n, 2 * inner // tiles)
        total = None
        for k in range(len(offsets) // 2):
            term = dot(x[:, columns_of(offsets[2 * k], pair)], held[k, :, at])
            total = term if total is None else total + term
        made[:, at] = total
        begin(n)

    each(tiles, step)
    finish()


def far_kernel(offsets, late, inner, *refs):
    source, group, blocks, out, x, part, held, down, hidden, made, *sems = take(
        refs, None, None, len(offsets)
    )
    core = lax.axis_index("expert") & 1
    whole = pltpu.make_async_copy(group, x, sems[0])
    whole.start()
    copies = load_pairs(
        [blocks[offsets.index(o)] for o in late], late, 0, 2 * inner, held, sems[1], core
    )
    tiles = tiles_of(inner // 2)
    tile = inner // tiles
    wait_part = columns_in(source, part, 2 * tiles, sems[2])
    later = load_pairs(blocks, offsets, 2 * inner, inner, down, sems[3], core)
    whole.wait()
    for copy in copies:
        copy.wait()
    pair = held.shape[1]

    def step(n):
        sums = []
        for base in (0, tiles):
            at = cut(base + n, tile)
            wait_part(base + n)
            total = part[:, at]
            for k in range(len(late) // 2):
                total = total + dot(x[:, columns_of(late[2 * k], pair)], held[k, :, at])
            sums.append(total)
        hidden[:, cut(n, tile)] = (jax.nn.silu(sums[0]) * sums[1]).astype(BF16)

    each(tiles, step)
    for copy in later:
        copy.wait()
    outs = []
    for k in range(len(offsets) // 2):
        at = columns_of(offsets[2 * k], pair)
        made[:, at] = dot_t(hidden[...], down[k])
        outs.append(pltpu.make_async_copy(made.at[:, at], out.at[:, at], sems[4].at[k]))
        outs[-1].start()
    for copy in outs:
        copy.wait()


def combine_kernel(count, parts, base, *refs):
    blocks, notes, source, outs, x, shared, made, *sems = take(refs, count, None, None, parts)
    wait_x = stack(blocks, x, sems[0])
    total, width = x.shape
    tiles = tiles_of(width)
    wait_shared = columns_in(source, shared, tiles, sems[1], base)
    rows = notes.shape[0]
    places = lax.broadcasted_iota(jnp.int32, (rows, total), 1)
    pick = (places == notes[:, 0:1].astype(jnp.int32)).astype(F32).astype(BF16)
    scale = notes[:, 1:2]
    wait_x()
    begin, finish = rows_out(made, outs, tiles, sems[2])

    def step(n):
        at = cut(n, width // tiles)
        routed = dot(pick, x[:, at])
        wait_shared(n)
        made[:, at] = (shared[:, at] + scale * routed).astype(BF16)
        begin(n)

    each(tiles, step)
    finish()


def call(kernel, ins, vmem, outs, scratch, flops, moved):
    return pl.pallas_call(
        kernel,
        out_shape=[jax.ShapeDtypeStruct(shape, kind) for shape, kind in outs],
        in_specs=[VMEM_SPEC if k in vmem else ANY_SPEC for k in range(len(ins))],
        out_specs=[ANY_SPEC] * len(outs),
        scratch_shapes=scratch,
        compiler_params=pltpu.CompilerParams(vmem_limit_bytes=VMEM_BYTES),
        cost_estimate=pl.CostEstimate(flops=flops, bytes_accessed=moved, transcendentals=0),
    )(*ins)


def dma(*shape):
    return pltpu.SemaphoreType.DMA(shape)


def pick_rows(own, got, slot, lengths):
    sources = [uses for _, uses in got]
    count, (rows, width) = lax.axis_size("tensor"), own.shape
    group, total = rows * count, sum(lengths)
    tiles = tiles_of(width)
    ins = [own, *[block for block, _ in got], slot[None, :]]
    out = call(
        functools.partial(pick_kernel, count, sources, lengths),
        ins,
        {len(ins) - 1},
        [((length, width), BF16) for length in lengths] + [((group, width), BF16)],
        [
            pltpu.VMEM((group, width), BF16),
            pltpu.VMEM((total, group), BF16),
            pltpu.VMEM((total, width), BF16),
            dma(count),
            dma(len(lengths), tiles),
            pltpu.SemaphoreType.DMA,
        ],
        2 * total * group * width,
        2 * (2 * group + total) * width,
    )
    return out[:-1], out[-1]


def expert_rows(blocks, w_gate, w_up, w_down):
    inner, width = w_down.shape[1:]
    rows, count = sum(b.shape[0] for b in blocks), len(blocks)
    ins, outs = tiles_of(inner // 2), width // part_tile(width)
    made = call(
        functools.partial(expert_kernel, count),
        [*blocks, w_gate, w_up, w_down],
        (),
        [((b.shape[0], wide), BF16) for _, wide in column_cuts(width) for b in blocks],
        [
            pltpu.VMEM((rows, width), BF16),
            pltpu.VMEM((width, inner), BF16),
            pltpu.VMEM((width, inner), BF16),
            pltpu.VMEM((inner, width), BF16),
            pltpu.VMEM((rows, inner), BF16),
            pltpu.VMEM((rows, width), BF16),
            dma(count),
            dma(ins),
            dma(ins),
            dma(outs),
            dma(PARTS, count, outs),
        ],
        6 * rows * inner * width,
        (4 * rows + 6 * inner) * width,
    )
    return [made[c * count:(c + 1) * count] for c in range(PARTS)]


def shared_near(group, blocks, inner):
    offsets = sorted(blocks)
    rows, (tokens, width) = blocks[0].shape[0], group.shape
    count = len(offsets)
    return call(
        functools.partial(near_kernel, offsets, inner),
        [group, *[blocks[o] for o in offsets]],
        (),
        [((tokens, 2 * inner), F32)],
        [
            pltpu.VMEM((tokens, width), BF16),
            pltpu.VMEM((count // 2, 2 * rows, 2 * inner), BF16),
            pltpu.VMEM((tokens, 2 * inner), F32),
            pltpu.SemaphoreType.DMA,
            dma(count),
            dma(1, tiles_of(2 * inner)),
        ],
        4 * tokens * inner * rows * count,
        4 * rows * inner * count + 8 * tokens * inner,
    )[0]


def shared_far(part, group, blocks, inner):
    offsets = sorted(blocks)
    late = [o for o in offsets if far(o)]
    rows, (tokens, width) = blocks[0].shape[0], group.shape
    count = len(offsets)
    return call(
        functools.partial(far_kernel, offsets, late, inner),
        [part, group, *[blocks[o] for o in offsets]],
        (),
        [((tokens, width), F32)],
        [
            pltpu.VMEM((tokens, width), BF16),
            pltpu.VMEM((tokens, 2 * inner), F32),
            pltpu.VMEM((len(late) // 2, 2 * rows, 2 * inner), BF16),
            pltpu.VMEM((count // 2, 2 * rows, inner), BF16),
            pltpu.VMEM((tokens, inner), BF16),
            pltpu.VMEM((tokens, width), F32),
            pltpu.SemaphoreType.DMA,
            dma(len(late)),
            dma(2 * tiles_of(inner // 2)),
            dma(count),
            dma(count // 2),
        ],
        4 * tokens * inner * rows * len(late) + 2 * tokens * inner * width,
        4 * rows * inner * len(late) + 6 * tokens * width + 8 * tokens * inner,
    )[0]


def combine(blocks, notes, shared, parts, base):
    group, width = shared.shape[0], blocks[0].shape[1]
    total = sum(b.shape[0] for b in blocks)
    tiles = tiles_of(width)
    ins = [*blocks, notes, shared]
    return call(
        functools.partial(combine_kernel, len(blocks), parts, base),
        ins,
        {len(blocks)},
        [((group // parts, width), BF16)] * parts,
        [
            pltpu.VMEM((total, width), BF16),
            pltpu.VMEM((group, width), F32),
            pltpu.VMEM((group, width), BF16),
            dma(len(blocks)),
            dma(tiles),
            dma(parts, tiles),
        ],
        2 * group * total * width,
        (2 * total + 6 * group) * width,
    )


def body(tokens, expert_ids, gates, w_gate, w_up, w_down, s_gate, s_up, s_down):
    size = lax.axis_size("expert")
    count = lax.axis_size("tensor")
    me = lax.axis_index("expert")
    place = lax.axis_index("tensor")
    rows, width = tokens.shape
    group = rows * count
    experts = w_gate.shape[0] * size
    cap = 2 * group // experts
    half = cap // 2
    inner = s_gate.shape[1]

    gathered = line_gather(tokens, count)
    s_all = jnp.concatenate([s_gate, s_up, s_down.T], axis=1)
    near = {bit: swap(s_all, "expert", bit) for bit in bits_of((size - 1) & ~1)}
    notes = jnp.concatenate([expert_ids.astype(F32).T, gates[None, :]], axis=0)
    others = [ring(notes, back) for back in range(1, count)]
    notes = jnp.concatenate([notes, *others], axis=1)
    ids, scale = notes[0].astype(jnp.int32), notes[1]

    index = jnp.arange(group, dtype=jnp.int32)
    back = index // rows
    index = jnp.where(back > place, place - back + count, place - back) * rows + index % rows
    same = (ids[:, None] == ids[None, :]) & (index[None, :] < index[:, None])
    spot = jnp.sum(same.astype(jnp.int32), axis=1)
    turned = spot + (place & 1) * half
    turned = jnp.where(turned >= cap, turned - cap, turned)
    base, lengths, total = [], [], 0
    for offset in range(size):
        lengths.append(half if far(offset) else cap)
        base.append(total)
        total += lengths[-1]
    slot = jnp.full((group,), -1, jnp.int32)
    for offset in range(size):
        value = base[offset] + spot
        if far(offset):
            value = jnp.where(turned < half, base[offset] + turned, -1)
        slot = jnp.where(ids ^ me == offset, value, slot)
    slot = lax.optimization_barrier(slot)
    fars = [o for o in range(size) if far(o)]
    nears = [o for o in range(2, size) if not far(o)]

    sent, tokens = pick_rows(tokens, gathered, slot, lengths)
    got = {0: sent[0]}
    for o in fars:
        got[o] = swap(sent[o], "expert", o)
    for o in nears:
        got[o] = swap(sent[o], "expert", o)
    got[1] = swap(sent[1], "expert", 1)
    blocks = with_partner({0: s_all, **near})
    part = None
    if 2 * s_all.shape[0] % LANES == 0:
        part = shared_near(tokens, blocks, inner)
    own = expert_rows([got[0], got[1]], w_gate, w_up, w_down)
    home = [{0: own[c][0]} for c in range(PARTS)]
    for c in range(PARTS):
        home[c][1] = swap(own[c][1], "expert", 1)
    mine = jnp.concatenate([got[o] for o in fars])
    mine, *ready = lax.optimization_barrier((mine, *near.values()))
    near = dict(zip(near, ready))
    other = swap(mine, "tensor", 1)
    late = far_blocks(near, s_all, size)
    made = expert_rows([mine, other], w_gate, w_up, w_down)
    pair = []
    for c in range(PARTS):
        pair.append((made[c][0], swap(made[c][1], "tensor", 1)))
    made = expert_rows([got[o] for o in nears], w_gate, w_up, w_down)
    for c in range(PARTS):
        mine = add(*pair[c])
        for k, o in enumerate(fars):
            home[c][o] = swap(mine[k * half:(k + 1) * half], "expert", o)
        for k, o in enumerate(nears):
            home[c][o] = swap(made[c][k], "expert", o)
    blocks = {**blocks, **with_partner(late)}

    if part is not None:
        shared = shared_far(part, tokens, blocks, inner)
    else:
        s_in = in_order({o: b[:, :2 * inner] for o, b in blocks.items()}, me)
        s_out = in_order({o: b[:, 2 * inner:] for o, b in blocks.items()}, me)
        pre = dot(tokens, s_in)
        shared = (jax.nn.silu(pre[:, :inner]) * pre[:, inner:]).astype(BF16)
        shared = dot_t(shared, s_out)

    notes = jnp.stack([slot.astype(F32), scale], axis=1)
    outs = []
    for c, (start, _) in enumerate(column_cuts(width)):
        parts = combine(
            [home[c][o] for o in range(size)], notes, shared, count, start
        )
        outs.append(line_scatter_staged(parts, place, count))
    return jnp.concatenate(outs, axis=1)


def solution(mesh):
    return jax.shard_map(
        body,
        mesh=mesh,
        in_specs=(
            P(("expert", "tensor"), None),
            P(("expert", "tensor"), None),
            P(("expert", "tensor")),
            P("expert", None, "tensor"),
            P("expert", None, "tensor"),
            P("expert", "tensor", None),
            P("expert", "tensor"),
            P("expert", "tensor"),
            P("tensor", "expert"),
        ),
        out_specs=P(("expert", "tensor"), None),
        check_vma=False,
    )
```
